512 devices in a mesh: users: 32 (over y, x, core), camps: 16 (over z).
Axes of the slice: x: 4, y: 4, z: 16, core: 2. Of those that a mesh axis runs over, the one named last changes fastest.
Arguments:
- scores: bfloat16 [64, 16, 12, 128, 128], P('users', 'camps'), may hold values from -12 to 12
- elig_ids: int32 [64, 16, 12], P('users', 'camps'), may hold values from 0 to 63, as said below
- elig_counts: int32 [64, 16], P('users', 'camps'), may hold values from 1 to 12, as said below
- activity: bfloat16 [24, 8192], P(None, 'users'), may hold values from 0.019897461 to 0.19921875
- prices: float32 [24, 131072], P(None, ('users', 'camps')), may hold values from 0 to 1.5
- spend_limit: float32 [24, 131072], P(None, ('users', 'camps')), may hold values from 3.072 to 16.896
Outputs:
- new_prices: float32 [24, 131072], P(None, ('users', 'camps'))
- direction: float32 [24, 131072], P(None, ('users', 'camps'))
The draws below stay inside these ranges and needn't reach their ends.
Inputs may be any that keep to these rules, and one draw needn't show every extreme that they name: `elig_ids`: the 12 numbers of each list are all different. `elig_counts`: in every campaign group some user block has 12 eligible slots.
All inputs are finite; a program needn't handle non-finite values.
Results may differ from the reference program's by a relative error of at most 0.008.
Values may be sent and summed in bfloat16 or wider, within the bound.
No kernel may reach another device: no remote copies, remote signals or barrier semaphores. Data moves between devices by JAX's collectives and lax.ppermute only.
A program may use at most 64 MiB of HBM per device.

```python
import math
import jax
import jax.numpy as jnp
from jax import lax

TILE = 128
HOURS = 24
KMAX = 12
STEPS = 2
CB_DEV = 64
UBLOCKS = 64
USERS = 8192
CAMPS = 131072
PIECE = 256
N_USERS = 32
N_CAMPS = 16


def draw_elig_ids(key, part):
    key = jax.random.fold_in(key, 11)
    keys = jax.random.randint(key, (UBLOCKS, N_CAMPS, CB_DEV), 0, 2 ** 30)
    order = jnp.argsort(keys, axis=-1, stable=True)
    return order[:, :, :KMAX].astype(jnp.int32)


def draw_elig_counts(key, part):
    key = jax.random.fold_in(key, 23)
    first, second = jax.random.split(key)
    counts = jax.random.randint(first, (UBLOCKS, N_CAMPS), 1, KMAX + 1)
    heavy = jax.random.randint(second, (N_CAMPS,), 0, UBLOCKS)
    rows = jnp.arange(UBLOCKS)[:, None]
    return jnp.where(rows == heavy[None, :], KMAX, counts).astype(jnp.int32)


def block_levels(key, shape, shards, smallest, top_value):
    loudness, own = 1.0, jax.random.fold_in(key, 6)
    for axis_at, blocks in shards:
        steps = jnp.exp(jax.random.uniform(jax.random.fold_in(own, axis_at), (blocks,), jnp.float32, smallest / len(shards), top_value / len(shards)))
        loudness = loudness * jnp.repeat(steps, shape[axis_at] // blocks).reshape([-1 if axis == axis_at else 1 for axis in range(len(shape))])
    return loudness


def scatter_about(rng, shape, scale, reach, shards=(), kind=jnp.bfloat16):
    result = scale * jax.random.normal(rng, shape, jnp.float32)
    if shards:
        result = result * block_levels(rng, shape, shards, -0.22, 0.18)
    return jnp.clip(result, -reach, reach).astype(kind)


def setup_inputs(seed: int = 0) -> dict:
    key_of = jax.random.split(jax.random.key(seed), 7)
    return {
        "scores": scatter_about(key_of[0], (UBLOCKS, N_CAMPS, KMAX, TILE, TILE), 2.0, 12.0, ((0, 32), (1, 16))),
        "elig_ids": draw_elig_ids(jax.random.fold_in(key_of[6], 71), 0),
        "elig_counts": draw_elig_counts(jax.random.fold_in(key_of[6], 71), 0),
        "activity": jnp.clip(jnp.exp(math.log(0.19921875) - 2.3038113 * jax.random.uniform(key_of[3], (HOURS, USERS), jnp.float32) ** block_levels(key_of[3], (HOURS, USERS), ((1, 32),), -0.2, 0.2)), 0.019897461, 0.19921875).astype(jnp.bfloat16),
        "prices": jnp.clip(1.5 * jax.random.uniform(key_of[4], (HOURS, CAMPS), jnp.float32) ** block_levels(key_of[4], (HOURS, CAMPS), ((1, 512),), -0.2, 0.2), 0.0, 1.5),
        "spend_limit": jnp.clip(3.072 + 13.823999881744385 * jax.random.uniform(key_of[5], (HOURS, CAMPS), jnp.float32) ** block_levels(key_of[5], (HOURS, CAMPS), ((1, 512),), -0.2, 0.2), 3.072, 16.896),
    }


def group_view(values):
    return values.reshape(HOURS, N_USERS, N_CAMPS, PIECE).transpose(0, 2, 1, 3).reshape(HOURS, N_CAMPS, CB_DEV * TILE)

def flat_view(values):
    return values.reshape(HOURS, N_CAMPS, N_USERS, PIECE).transpose(0, 2, 1, 3).reshape(HOURS, CAMPS)

def usage_of(lam_group, scores, elig_ids, elig_counts, activity):
    rounded = lax.optimization_barrier(lam_group.astype(jnp.bfloat16))
    table = rounded.astype(jnp.float32).reshape(HOURS, N_CAMPS, CB_DEV, TILE).transpose(1, 0, 2, 3)
    acts = activity.astype(jnp.float32).reshape(HOURS, UBLOCKS, TILE).transpose(1, 0, 2)
    columns = jnp.arange(CB_DEV, dtype=jnp.int32)
    slot_ids = jnp.arange(KMAX, dtype=jnp.int32)

    def one_block(total, inputs):
        act_b, tile_b, ids_b, count_b = inputs
        picked = jax.vmap(lambda tab, idx: jnp.take(tab, idx, axis=1))(table, ids_b)
        cost = jnp.einsum('hu,chkt->ckut', act_b, picked)
        live = (slot_ids[None, :] < count_b[:, None]).astype(jnp.float32)
        share = jnp.clip(0.5 + (tile_b.astype(jnp.float32) - cost) / 2.0, 0.0, 1.0) * live[:, :, None, None]
        share = lax.optimization_barrier(share.astype(jnp.bfloat16)).astype(jnp.float32)
        used = jnp.einsum('hu,ckut->chkt', act_b, share)
        onehot = (ids_b[:, :, None] == columns[None, None, :]).astype(jnp.float32)
        return (total + jnp.einsum('chkt,ckn->chnt', used, onehot), None)
    init = jnp.zeros((N_CAMPS, HOURS, CB_DEV, TILE), jnp.float32)
    total, _ = lax.scan(one_block, init, (acts, scores, elig_ids, elig_counts))
    return total.transpose(1, 0, 2, 3).reshape(HOURS, N_CAMPS, CB_DEV * TILE)

def reference(scores, elig_ids, elig_counts, activity, prices, spend_limit):
    anchor = group_view(prices)
    limit_group = group_view(spend_limit)
    entries = HOURS * CAMPS

    def direction_at(lam):
        gap = usage_of(lam, scores, elig_ids, elig_counts, activity) - limit_group
        squares = jnp.sum(gap * gap)
        return gap * lax.rsqrt(squares / entries + 1e-06)
    lam = anchor
    last = anchor
    for step in range(STEPS):
        middle = jnp.maximum(lam + 0.3 * direction_at(lam), 0.0)
        last = direction_at(middle)
        extra = jnp.maximum(lam + 0.3 * last, 0.0)
        weight = 1.0 / (step + 2.0)
        lam = weight * anchor + (1.0 - weight) * extra
    return (flat_view(lam), flat_view(last))
```

```python
import functools

import jax
import jax.numpy as jnp
from jax import lax
from jax.experimental import pallas as pl
from jax.experimental.pallas import tpu as pltpu
from jax.sharding import Mesh
from jax.sharding import PartitionSpec as P

STEPS = 2
USERS = ("users_0", "users_1", "users_2")
USERS_CAMPS = ("users_0", "users_1", "users_2", "camps")
TILE = 128
ACT = 32
FLAGS = 8
UNROLL = 4

VMEM = pl.BlockSpec(memory_space=pltpu.VMEM)
SMEM = pl.BlockSpec(memory_space=pltpu.SMEM)


def packet_rows(blocks, owned):
    return blocks * owned * TILE + blocks * ACT + FLAGS


def pack_kernel(owned, ids_ref, counts_ref, scores_ref, act_ref, out_ref):
    devices = out_ref.shape[0]
    hours = act_ref.shape[0]
    blocks, slots = scores_ref.shape[0], scores_ref.shape[1]
    acts = blocks * owned * TILE
    flags = acts + blocks * ACT
    hour = lax.broadcasted_iota(jnp.int32, (ACT - hours, TILE), 0)
    ones = jnp.where(hour == 0, 1.0, 0.0).astype(jnp.bfloat16)
    lane = lax.broadcasted_iota(jnp.int32, (FLAGS, TILE), 1)
    tails = [
        jnp.concatenate([act_ref[:, b * TILE : (b + 1) * TILE], ones], axis=0)
        for b in range(blocks)
    ]
    for dev in range(devices):
        for b in range(blocks):
            out_ref[dev, acts + b * ACT : acts + (b + 1) * ACT, :] = tails[b]
        out_ref[dev, flags : flags + FLAGS, :] = jnp.zeros((FLAGS, TILE), jnp.bfloat16)

    for b in range(blocks):

        @pl.loop(0, jnp.minimum(counts_ref[b], slots))
        def _(k):
            where = ids_ref[b, k]
            dev = where // owned
            slot = b * owned + lax.rem(where, owned)
            row = pl.multiple_of(slot * TILE, TILE)
            out_ref[dev, pl.ds(row, TILE), :] = scores_ref[b, k]
            mark = jnp.where(lane == slot, 1.0, 0.0).astype(jnp.bfloat16)
            out_ref[dev, flags : flags + FLAGS, :] += mark


def list_kernel(blocks, owned, flags_ref, list_ref):
    devices = flags_ref.shape[0]
    span = list_ref.shape[1]
    for t in range(owned):

        def add(i, n, t=t):
            for b in range(blocks):
                list_ref[t, n + 1] = i * blocks + b
                n = n + flags_ref[i, b * owned + t]
            return n

        n = lax.fori_loop(0, devices, add, jnp.int32(0))
        last = list_ref[t, jnp.maximum(n, 1)]
        for p in range(UNROLL):
            list_ref[t, jnp.minimum(n + 1 + p, span - 1)] = last
        list_ref[t, 0] = n


def local_usage(owned, lam, list_ref, packets_ref):
    hours = lam.shape[0]
    rows = packets_ref.shape[1]
    blocks = (rows - FLAGS) // (owned * TILE + ACT)
    acts = blocks * owned * TILE
    hour = lax.broadcasted_iota(jnp.int32, (ACT - hours, TILE), 0)
    half = jnp.where(hour == 0, 0.5, 0.0).astype(jnp.bfloat16)
    usages = []
    for t in range(owned):
        rounded = lam[:, t * TILE : (t + 1) * TILE].astype(jnp.bfloat16)
        weights = jnp.concatenate([rounded * jnp.bfloat16(-0.5), half], axis=0)
        count = list_ref[t, 0]

        def group(g, total, t=t, weights=weights, count=count):
            for p in range(UNROLL):
                at = g * UNROLL + p
                entry = list_ref[t, at + 1]
                dev = entry // blocks
                b = lax.rem(entry, blocks)
                act_row = pl.multiple_of(acts + b * ACT, ACT)
                act = packets_ref[dev, pl.ds(act_row, ACT), :]
                row = pl.multiple_of((b * owned + t) * TILE, TILE)
                score = packets_ref[dev, pl.ds(row, TILE), :].astype(jnp.float32)
                part = lax.dot_general(
                    act, weights, (((0,), (0,)), ((), ())), preferred_element_type=jnp.float32
                )
                share = jnp.clip(score * 0.5 + part, 0.0, 1.0).astype(jnp.bfloat16)
                live = jnp.where(at < count, 1.0, 0.0).astype(jnp.bfloat16)
                total = total + jnp.dot(act * live, share, preferred_element_type=jnp.float32)
            return total

        groups = (count + UNROLL - 1) // UNROLL
        total = lax.fori_loop(0, groups, group, jnp.zeros((ACT, TILE), jnp.float32))
        usages.append(total[:hours])
    return jnp.concatenate(usages, axis=1)


def scale_of(parts_ref, entries):
    squares = jnp.sum(jnp.sum(parts_ref[:, 0, :], axis=0, keepdims=True), axis=1, keepdims=True)
    return lax.rsqrt(squares / entries + 1e-06)


def moved(lam, gap, scale):
    return jnp.maximum(lam + 0.3 * (gap * scale), 0.0)


def direction_kernel(owned, entries, kind, *refs):
    if kind == "first":
        list_ref, packets_ref, limit_ref, lam_ref, gap_ref, parts_ref = refs
        at = lam_ref[...]
    elif kind == "middle":
        list_ref, packets_ref, limit_ref, lam_ref, before_ref, sums_ref, gap_ref, parts_ref = refs
        at = moved(lam_ref[...], before_ref[...], scale_of(sums_ref, entries))
    else:
        (list_ref, packets_ref, limit_ref, anchor_ref, lam_ref, before_ref, sums_ref) = refs[:7]
        gap_ref, parts_ref, lam_out_ref = refs[7:]
        extra = moved(lam_ref[...], before_ref[...], scale_of(sums_ref, entries))
        weight = 1.0 / (kind + 2.0)
        at = weight * anchor_ref[...] + (1.0 - weight) * extra
        lam_out_ref[...] = at
    gap = local_usage(owned, at, list_ref, packets_ref) - limit_ref[...]
    gap_ref[...] = gap
    squares = gap * gap
    line = sum(squares[:, t * TILE : (t + 1) * TILE] for t in range(owned))
    line = jnp.sum(line, axis=0, keepdims=True)
    parts_ref[...] = jnp.broadcast_to(line[None], parts_ref.shape)


def final_kernel(entries, step, anchor_ref, lam_ref, gap_ref, sums_ref, new_ref, dir_ref):
    scale = scale_of(sums_ref, entries)
    gap = gap_ref[...]
    dir_ref[...] = gap * scale
    extra = moved(lam_ref[...], gap, scale)
    weight = 1.0 / (step + 2.0)
    new_ref[...] = weight * anchor_ref[...] + (1.0 - weight) * extra


def swapped(parts, axis):
    return lax.all_to_all(parts, axis, split_axis=0, concat_axis=0, tiled=True)


def on_device(scores, elig_ids, elig_counts, activity, prices, spend_limit):
    devices = lax.axis_size(USERS)
    groups = lax.axis_size("camps")
    entries = float(prices.size * devices * groups)
    hours, piece = prices.shape
    owned = piece // TILE
    blocks = scores.shape[0]
    rows = packet_rows(blocks, owned)
    params = pltpu.CompilerParams(vmem_limit_bytes=8 * 2**20)

    packets = pl.pallas_call(
        functools.partial(pack_kernel, owned),
        out_shape=jax.ShapeDtypeStruct((devices, rows, TILE), jnp.bfloat16),
        in_specs=[SMEM, SMEM, VMEM, VMEM],
        out_specs=VMEM,
        compiler_params=params,
        name="pack",
    )(elig_ids[:, 0], elig_counts[:, 0], scores[:, 0], activity)
    packets = swapped(packets, USERS)
    flags = packets[:, rows - FLAGS, : blocks * owned].astype(jnp.int32)
    lists = pl.pallas_call(
        functools.partial(list_kernel, blocks, owned),
        out_shape=jax.ShapeDtypeStruct((owned, devices * blocks + 1 + UNROLL), jnp.int32),
        in_specs=[SMEM],
        out_specs=SMEM,
        compiler_params=params,
        name="lists",
    )(flags)

    value = jax.ShapeDtypeStruct(prices.shape, jnp.float32)
    parts = jax.ShapeDtypeStruct((devices, 1, TILE), jnp.float32)

    def direction(kind, *args):
        outs = [value, parts] + ([value] if kind not in ("first", "middle") else [])
        got = pl.pallas_call(
            functools.partial(direction_kernel, owned, entries, kind),
            out_shape=outs,
            in_specs=[SMEM] + [VMEM] * (len(args) + 2),
            out_specs=[VMEM] * len(outs),
            compiler_params=params,
            name="direction",
        )(lists, packets, spend_limit, *args)
        over_users = swapped(got[1], USERS).sum(axis=0)
        sums = swapped(jnp.broadcast_to(over_users[None], (groups, 1, TILE)), "camps")
        return got[0], sums, got[2:]

    lam = prices
    gap, sums, _ = direction("first", lam)
    for step in range(STEPS):
        gap, sums, _ = direction("middle", lam, gap, sums)
        if step < STEPS - 1:
            gap, sums, (lam,) = direction(step, prices, lam, gap, sums)
    new, last = pl.pallas_call(
        functools.partial(final_kernel, entries, STEPS - 1),
        out_shape=[value, value],
        in_specs=[VMEM] * 4,
        out_specs=[VMEM] * 2,
        compiler_params=params,
        name="final",
    )(prices, lam, gap, sums)
    return (new, last)


def solution(mesh):
    torus = Mesh(
        mesh.devices.reshape(4, 4, 2, mesh.shape["camps"]),
        ("users_0", "users_1", "users_2", "camps"),
    )
    in_specs = (
        P(USERS, "camps", None, None, None),
        P(USERS, "camps", None),
        P(USERS, "camps"),
        P(None, USERS),
        P(None, USERS_CAMPS),
        P(None, USERS_CAMPS),
    )
    out_specs = (P(None, USERS_CAMPS), P(None, USERS_CAMPS))
    return jax.shard_map(
        on_device, mesh=torus, in_specs=in_specs, out_specs=out_specs, check_vma=False
    )
```

```python
import functools

import jax
import jax.numpy as jnp
from jax import lax
from jax.experimental import pallas as pl
from jax.experimental.pallas import tpu as pltpu
from jax.sharding import Mesh
from jax.sharding import PartitionSpec as P

STEPS = 2
USERS = ("users_0", "users_1", "users_2")
USERS_CAMPS = ("users_0", "users_1", "users_2", "camps")
TILE = 128
FLAGS = 8
GROUP = 8
HOT = 3
ACT = 32

VMEM = pl.BlockSpec(memory_space=pltpu.VMEM)
SMEM = pl.BlockSpec(memory_space=pltpu.SMEM)
HBM = pl.BlockSpec(memory_space=pl.ANY)


def pack_kernel(owned, ids_hbm, counts_hbm, scores_hbm, act_hbm, out_ref, ids, counts, scores, act, sems):
    copies = [
        pltpu.make_async_copy(src, dst, sems.at[n])
        for n, (src, dst) in enumerate(
            ((ids_hbm, ids), (counts_hbm, counts), (act_hbm, act), (scores_hbm, scores))
        )
    ]
    for copy in copies:
        copy.start()
    devices = out_ref.shape[0]
    hours = act.shape[0]
    blocks, slots = scores.shape[0], scores.shape[2]
    acts = blocks * owned * TILE
    flags = acts + blocks * hours
    lane = lax.broadcasted_iota(jnp.int32, (FLAGS, TILE), 1)
    for dev in range(devices):
        out_ref[dev, flags : flags + FLAGS, :] = jnp.zeros((FLAGS, TILE), jnp.bfloat16)
    copies[2].wait()
    for b in range(blocks):
        own = act[:, b * TILE : (b + 1) * TILE]
        for dev in range(devices):
            out_ref[dev, acts + b * hours : acts + (b + 1) * hours, :] = own
    copies[0].wait()
    copies[1].wait()
    copies[3].wait()
    for b in range(blocks):

        @pl.loop(0, jnp.minimum(counts[b], slots))
        def _(k):
            where = ids[b, 0, k]
            dev = where // owned
            slot = b * owned + lax.rem(where, owned)
            row = pl.multiple_of(slot * TILE, TILE)
            out_ref[dev, pl.ds(row, TILE), :] = scores[b, 0, k] * jnp.bfloat16(0.5)
            mark = jnp.where(lane == slot, 1.0, 0.0).astype(jnp.bfloat16)
            out_ref[dev, flags : flags + FLAGS, :] += mark


def collect(hours, owned, blocks, flags_ref, packets_ref, counts_ref, tiles, acts, far_tiles, far_acts, order, near, sems):
    devices = packets_ref.shape[0]
    act_rows = blocks * owned * TILE
    first = GROUP * HOT
    hour = lax.broadcasted_iota(jnp.int32, (ACT - hours, TILE), 0)
    tail = jnp.where(hour == 0, 1.0, 0.0).astype(jnp.bfloat16)
    counts = []
    for t in range(owned):
        n = jnp.int32(0)
        for i in range(devices):
            for b in range(blocks):
                order[t, n] = i * blocks + b
                n = n + flags_ref[i, b * owned + t]
        counts.append(n)
        counts_ref[t] = n
    most = functools.reduce(jnp.maximum, counts)
    full = jnp.minimum((most + GROUP - 1) // GROUP, HOT) * GROUP

    def lines(t, p):
        entry = order[t, p]
        dev = entry // blocks
        b = lax.rem(entry, blocks)
        row = pl.multiple_of((b * owned + t) * TILE, TILE)
        act_row = pl.multiple_of(act_rows + b * hours, 8)
        tile = packets_ref[dev, pl.ds(row, TILE), :]
        act = packets_ref[dev, pl.ds(act_row, hours), :]
        return tile, jnp.concatenate([act, tail], axis=0)

    def keep(t, p, tile, act):
        g, at = p // GROUP, pl.multiple_of(lax.rem(p, GROUP) * TILE, TILE)
        tiles[t, g, pl.ds(at, TILE), :] = tile
        acts[t, g, :, pl.ds(at, TILE)] = act

    for t in range(owned):

        @pl.loop(0, jnp.minimum(counts[t], first))
        def _(p, t=t):
            keep(t, p, *lines(t, p))

        @pl.loop(jnp.minimum(counts[t], first), full)
        def _(p, t=t):
            keep(t, p, jnp.zeros((TILE, TILE), jnp.bfloat16), jnp.zeros((ACT, TILE), jnp.bfloat16))

        @pl.loop(first, counts[t])
        def _(p, t=t):
            tile, act = lines(t, p)
            near[:TILE] = tile
            near[TILE:] = act
            for n, (src, dst) in enumerate(((near.at[:TILE], far_tiles), (near.at[TILE:], far_acts))):
                copy = pltpu.make_async_copy(src, dst.at[t, p - first], sems.at[n])
                copy.start()
                copy.wait()


def local_usage(owned, lam, counts_ref, tiles, acts, far_tiles, far_acts, near, sems):
    hours = lam.shape[0]
    first = GROUP * HOT
    hour = lax.broadcasted_iota(jnp.int32, (ACT - hours, TILE), 0)
    half = jnp.where(hour == 0, 0.5, 0.0).astype(jnp.bfloat16)
    weights = []
    for t in range(owned):
        rounded = lam[:, t * TILE : (t + 1) * TILE].astype(jnp.bfloat16)
        weights.append(jnp.concatenate([rounded * jnp.bfloat16(-0.5), half], axis=0))
    most = functools.reduce(jnp.maximum, [counts_ref[t] for t in range(owned)])

    def used(t, tile, act):
        part = lax.dot_general(
            act, weights[t], (((0,), (0,)), ((), ())), preferred_element_type=jnp.float32
        )
        share = jnp.clip(tile.astype(jnp.float32) + part, 0.0, 1.0).astype(jnp.bfloat16)
        return jnp.dot(act, share, preferred_element_type=jnp.float32)

    def group(g, totals):
        return tuple(totals[t] + used(t, tiles[t, g], acts[t, g]) for t in range(owned))

    def further(t, p, total):
        for n, (src, dst) in enumerate(((far_tiles, near.at[:TILE]), (far_acts, near.at[TILE:]))):
            copy = pltpu.make_async_copy(src.at[t, p - first], dst, sems.at[n])
            copy.start()
            copy.wait()
        return total + used(t, near[:TILE], near[TILE:])

    zeros = tuple(jnp.zeros((ACT, TILE), jnp.float32) for _ in range(owned))
    groups = jnp.minimum((most + GROUP - 1) // GROUP, HOT)
    totals = lax.fori_loop(0, groups, group, zeros)
    totals = [
        lax.fori_loop(first, jnp.maximum(counts_ref[t], first), functools.partial(further, t), totals[t])
        for t in range(owned)
    ]
    return jnp.concatenate([total[:hours] for total in totals], axis=1)


def scale_of(parts_ref, entries):
    squares = jnp.sum(jnp.sum(parts_ref[:, 0, :], axis=0, keepdims=True), axis=1, keepdims=True)
    return lax.rsqrt(squares / entries + 1e-06)


def moved(lam, gap, scale):
    return jnp.maximum(lam + 0.3 * (gap * scale), 0.0)


def direction_kernel(owned, blocks, entries, kind, *refs):
    if kind == "first":
        flags_ref, packets_ref, limit_ref, lam_ref, gap_ref, parts_ref, counts_ref = refs[:7]
        store = refs[7:11]
        near, sems, order = refs[11:]
        at = lam_ref[...]
        collect(at.shape[0], owned, blocks, flags_ref, packets_ref, counts_ref, *store, order, near, sems)
    else:
        counts_ref, store, limit_ref = refs[0], refs[1:5], refs[5]
        near, sems = refs[-2:]
        refs = refs[6:-2]
        if kind == "middle":
            lam_ref, before_ref, sums_ref, gap_ref, parts_ref = refs
            at = moved(lam_ref[...], before_ref[...], scale_of(sums_ref, entries))
        else:
            anchor_ref, lam_ref, before_ref, sums_ref, gap_ref, parts_ref, lam_out_ref = refs
            extra = moved(lam_ref[...], before_ref[...], scale_of(sums_ref, entries))
            weight = 1.0 / (kind + 2.0)
            at = weight * anchor_ref[...] + (1.0 - weight) * extra
            lam_out_ref[...] = at
    gap = local_usage(owned, at, counts_ref, *store, near, sems) - limit_ref[...]
    gap_ref[...] = gap
    squares = gap * gap
    line = sum(squares[:, t * TILE : (t + 1) * TILE] for t in range(owned))
    line = jnp.sum(line, axis=0, keepdims=True)
    parts_ref[...] = jnp.broadcast_to(line[None], parts_ref.shape)


def fold_kernel(parts_ref, out_ref):
    line = jnp.sum(parts_ref[:, 0, :], axis=0, keepdims=True)
    out_ref[...] = jnp.broadcast_to(line[None], out_ref.shape)


def final_kernel(entries, step, anchor_ref, lam_ref, gap_ref, sums_ref, new_ref, dir_ref):
    scale = scale_of(sums_ref, entries)
    gap = gap_ref[...]
    dir_ref[...] = gap * scale
    extra = moved(lam_ref[...], gap, scale)
    weight = 1.0 / (step + 2.0)
    new_ref[...] = weight * anchor_ref[...] + (1.0 - weight) * extra


def swapped(parts, axis):
    return lax.all_to_all(parts, axis, split_axis=0, concat_axis=0, tiled=True)


def on_device(scores, elig_ids, elig_counts, activity, prices, spend_limit):
    devices = lax.axis_size(USERS)
    groups = lax.axis_size("camps")
    entries = float(prices.size * devices * groups)
    hours, piece = prices.shape
    owned = piece // TILE
    blocks = scores.shape[0]
    rows = blocks * owned * TILE + blocks * hours + FLAGS
    far = max(devices * blocks - GROUP * HOT, 1)
    params = pltpu.CompilerParams(vmem_limit_bytes=8 * 2**20)

    packets = pl.pallas_call(
        functools.partial(pack_kernel, owned),
        out_shape=jax.ShapeDtypeStruct((devices, rows, TILE), jnp.bfloat16),
        in_specs=[HBM] * 4,
        out_specs=VMEM,
        scratch_shapes=[
            pltpu.SMEM(elig_ids.shape, jnp.int32),
            pltpu.SMEM((blocks,), jnp.int32),
            pltpu.VMEM(scores.shape, jnp.bfloat16),
            pltpu.VMEM(activity.shape, jnp.bfloat16),
            pltpu.SemaphoreType.DMA((4,)),
        ],
        compiler_params=params,
        name="pack",
    )(elig_ids, elig_counts[:, 0], scores, activity)
    packets = swapped(packets, USERS)
    flags = packets[:, rows - FLAGS, : blocks * owned].astype(jnp.int32)

    value = jax.ShapeDtypeStruct(prices.shape, jnp.float32)
    parts = jax.ShapeDtypeStruct((devices, 1, TILE), jnp.float32)
    scratch = [pltpu.VMEM((TILE + ACT, TILE), jnp.bfloat16), pltpu.SemaphoreType.DMA((2,))]
    store_shapes = [
        jax.ShapeDtypeStruct((owned, HOT, GROUP * TILE, TILE), jnp.bfloat16),
        jax.ShapeDtypeStruct((owned, HOT, ACT, GROUP * TILE), jnp.bfloat16),
        jax.ShapeDtypeStruct((owned, far, TILE, TILE), jnp.bfloat16),
        jax.ShapeDtypeStruct((owned, far, ACT, TILE), jnp.bfloat16),
    ]
    store_specs = [VMEM, VMEM, HBM, HBM]

    def total_of(part):
        over_users = pl.pallas_call(
            fold_kernel,
            out_shape=jax.ShapeDtypeStruct((groups, 1, TILE), jnp.float32),
            in_specs=[VMEM],
            out_specs=VMEM,
            compiler_params=params,
            name="fold",
        )(swapped(part, USERS))
        return swapped(over_users, "camps")

    def call(kind, ins, outs, in_specs, out_specs, scratch_shapes):
        return pl.pallas_call(
            functools.partial(direction_kernel, owned, blocks, entries, kind),
            out_shape=outs,
            in_specs=in_specs,
            out_specs=out_specs,
            scratch_shapes=scratch_shapes,
            compiler_params=params,
            name="direction",
        )(*ins)

    got = call(
        "first",
        (flags, packets, spend_limit, prices),
        [value, parts, jax.ShapeDtypeStruct((owned,), jnp.int32)] + store_shapes,
        [SMEM] + [VMEM] * 3,
        [VMEM, VMEM, SMEM] + store_specs,
        scratch + [pltpu.SMEM((owned, devices * blocks), jnp.int32)],
    )
    gap, sums, kept = got[0], total_of(got[1]), got[2:]

    def direction(kind, *args):
        outs = [value, parts] + ([value] if kind != "middle" else [])
        got = call(
            kind,
            (*kept, spend_limit, *args),
            outs,
            [SMEM] + store_specs + [VMEM] * (len(args) + 1),
            [VMEM] * len(outs),
            scratch,
        )
        return got[0], total_of(got[1]), got[2:]

    lam = prices
    for step in range(STEPS):
        gap, sums, _ = direction("middle", lam, gap, sums)
        if step < STEPS - 1:
            gap, sums, (lam,) = direction(step, prices, lam, gap, sums)
    new, last = pl.pallas_call(
        functools.partial(final_kernel, entries, STEPS - 1),
        out_shape=[value, value],
        in_specs=[VMEM] * 4,
        out_specs=[VMEM] * 2,
        compiler_params=params,
        name="final",
    )(prices, lam, gap, sums)
    return (new, last)


def solution(mesh):
    torus = Mesh(
        mesh.devices.reshape(4, 4, 2, mesh.shape["camps"]),
        ("users_0", "users_1", "users_2", "camps"),
    )
    in_specs = (
        P(USERS, "camps", None, None, None),
        P(USERS, "camps", None),
        P(USERS, "camps"),
        P(None, USERS),
        P(None, USERS_CAMPS),
        P(None, USERS_CAMPS),
    )
    out_specs = (P(None, USERS_CAMPS), P(None, USERS_CAMPS))
    return jax.shard_map(
        on_device, mesh=torus, in_specs=in_specs, out_specs=out_specs, check_vma=False
    )
```

```python
import functools

import jax
import jax.numpy as jnp
from jax import lax
from jax.experimental import pallas as pl
from jax.experimental.pallas import tpu as pltpu
from jax.sharding import Mesh
from jax.sharding import PartitionSpec as P

STEPS = 2
USERS = ("users_0", "users_1", "users_2")
USERS_CAMPS = ("users_0", "users_1", "users_2", "camps")
TILE = 128
LINES = 8
LIST = 19
GROUP = 8
ACT = 32

VMEM = pl.BlockSpec(memory_space=pltpu.VMEM)
SMEM = pl.BlockSpec(memory_space=pltpu.SMEM)
HBM = pl.BlockSpec(memory_space=pltpu.HBM)
PARAMS = pltpu.CompilerParams(vmem_limit_bytes=8 * 2**20)


def copied(src, dst, sem):
    copy = pltpu.make_async_copy(src, dst, sem)
    copy.start()
    copy.wait()


def cut_kernel(ids_ref, scores_hbm, act_hbm, out_ref, scores, act, sems):
    load_act = pltpu.make_async_copy(act_hbm, act, sems.at[0])
    load_scores = pltpu.make_async_copy(scores_hbm, scores, sems.at[1])
    load_act.start()
    load_scores.start()
    devices = out_ref.shape[0]
    hours = act.shape[0]
    blocks, slots = scores.shape[0], scores.shape[2]
    piece = TILE * blocks // devices
    acts = slots * piece
    lines = acts + blocks * hours
    ids = ids_ref[...]
    for dev in range(devices):
        out_ref[dev, lines : lines + LINES, :] = ids
    load_act.wait()
    for b in range(blocks):
        own = act[:, b * TILE : (b + 1) * TILE]
        for dev in range(devices):
            out_ref[dev, acts + b * hours : acts + (b + 1) * hours, :] = own
    load_scores.wait()
    for b in range(blocks):
        for k in range(slots):
            for q in range(devices // blocks):
                rows = scores[b, 0, k, q * piece : (q + 1) * piece, :] * jnp.bfloat16(0.5)
                out_ref[q * blocks + b, k * piece : (k + 1) * piece, :] = rows


def route_kernel(owned, slots, which_ref, *refs):
    ids_refs, packets_ref = refs[:-8], refs[-8]
    out_ref, longest_ref = refs[-7:-5]
    places, where, sem = refs[-3:]
    blocks = len(ids_refs)
    devices = packets_ref.shape[0]
    piece = TILE * blocks // devices
    shape = (devices, TILE)
    lane = lax.broadcasted_iota(jnp.int32, shape, 1)
    source = lax.broadcasted_iota(jnp.int32, (devices, 1), 0)
    which = which_ref[0]

    def owner_is(ids, k):
        column = ids[:, k : k + 1]
        return column, jnp.where(column < 0, -1, column // owned) == lane

    longest = jnp.float32(0.0)
    for ids_ref in ids_refs:
        held = jnp.zeros(shape, jnp.float32)
        for k in range(slots):
            held += owner_is(ids_ref[...], k)[1].astype(jnp.float32)
        longest = jnp.maximum(longest, jnp.max(jnp.sum(held, axis=0, keepdims=True)))
    longest_ref[0] = longest.astype(jnp.int32)

    mine = ids_refs[0][...]
    for b in range(1, blocks):
        mine = jnp.where(which == b, ids_refs[b][...], mine)
    held = jnp.zeros(shape, jnp.float32)
    hits = []
    for k in range(slots):
        column, hit = owner_is(mine, k)
        hits.append((column, hit.astype(jnp.float32)))
        held += hits[-1][1]
    row = lax.broadcasted_iota(jnp.int32, (devices, devices), 0)
    col = lax.broadcasted_iota(jnp.int32, (devices, devices), 1)
    before = jnp.where(col < row, 1.0, 0.0).astype(jnp.bfloat16)
    ranks = jnp.dot(before, held.astype(jnp.bfloat16), preferred_element_type=jnp.float32)
    place = jnp.zeros(shape, jnp.int32)
    notes = jnp.zeros((TILE, TILE), jnp.float32)
    for k in range(slots):
        column, hit = hits[k]
        rank = jnp.sum(hit * ranks, axis=1, keepdims=True).astype(jnp.int32)
        ranks += hit
        live = jnp.logical_and(column >= 0, rank < LIST)
        spot = jnp.where(live, column // owned * (LIST + 1) + rank, LIST)
        place = jnp.where(lane == k, spot, place)
        code = (source * owned + lax.rem(column, owned) + 1).astype(jnp.float32)
        note = jnp.where(jnp.logical_and(lane == rank, live), code, 0.0)
        notes += lax.dot_general(
            hit.astype(jnp.bfloat16),
            note.astype(jnp.bfloat16),
            (((0,), (0,)), ((), ())),
            preferred_element_type=jnp.float32,
        )
    places[...] = place
    copied(places, where, sem)

    @pl.loop(0, devices)
    def _(i):
        for k in range(slots):
            out_ref[where[i, k]] = packets_ref[i, k * piece : (k + 1) * piece, :]

    for j in range(devices):
        note = jnp.broadcast_to(notes[j : j + 1, :], (piece, TILE))
        out_ref[j * (LIST + 1) + LIST] = note.astype(jnp.bfloat16)


def pack_kernel(owned, ids, counts, scores, act, out_ref):
    devices = out_ref.shape[0]
    hours = act.shape[0]
    blocks, slots = scores.shape[0], scores.shape[2]
    acts = blocks * owned * TILE
    flags = acts + blocks * hours
    lane = lax.broadcasted_iota(jnp.int32, (LINES, TILE), 1)

    @pl.loop(0, devices)
    def _(dev):
        out_ref[dev, flags : flags + LINES, :] = jnp.zeros((LINES, TILE), jnp.bfloat16)
        for b in range(blocks):
            own = act[:, b * TILE : (b + 1) * TILE]
            out_ref[dev, acts + b * hours : acts + (b + 1) * hours, :] = own

    for b in range(blocks):

        @pl.loop(0, jnp.minimum(counts[b], slots))
        def _(k):
            at = ids[b, 0, k]
            dev = at // owned
            slot = b * owned + lax.rem(at, owned)
            row = pl.multiple_of(slot * TILE, TILE)
            out_ref[dev, pl.ds(row, TILE), :] = scores[b, 0, k] * jnp.bfloat16(0.5)
            mark = jnp.where(lane == slot, (k + 1).astype(jnp.float32), 0.0)
            out_ref[dev, flags : flags + LINES, :] += mark.astype(jnp.bfloat16)


def activity_rows(act):
    hour = lax.broadcasted_iota(jnp.int32, (ACT - act.shape[0], TILE), 0)
    return jnp.concatenate([act, jnp.where(hour == 0, 1.0, 0.0).astype(jnp.bfloat16)], axis=0)


def far_kernel(hours, owned, blocks, flags_ref, packets_ref, far_tiles, far_acts, counts_ref, near, sem):
    devices = packets_ref.shape[0]
    acts = blocks * owned * TILE
    for t in range(owned):
        counts_ref[t] = 0
    for b in range(blocks):

        @pl.loop(0, devices, init_carry=jnp.int32(0))
        def _(i, taken, b=b):
            flags = [flags_ref[i, b * owned + t] for t in range(owned)]
            for t in range(owned):
                rank = taken
                for flag in flags:
                    rank += jnp.logical_and(flag > 0, flag < flags[t]).astype(jnp.int32)

                @pl.when(jnp.logical_and(flags[t] > 0, rank >= LIST))
                def _(t=t):
                    n = counts_ref[t]
                    slot = b * owned + t
                    near[:TILE] = packets_ref[i, slot * TILE : (slot + 1) * TILE, :]
                    rows = packets_ref[i, acts + b * hours : acts + (b + 1) * hours, :]
                    near[TILE:] = activity_rows(rows)
                    copied(near.at[:TILE], far_tiles.at[t, n], sem)
                    copied(near.at[TILE:], far_acts.at[t, n], sem)
                    counts_ref[t] = n + 1

            return taken + sum((flag > 0).astype(jnp.int32) for flag in flags)


def collect(hours, owned, blocks, notes_ref, far_counts_ref, packets_ref, lists_ref, counts_ref, tiles, acts, order):
    devices = packets_ref.shape[0]
    piece = TILE * blocks // devices
    act_rows = packets_ref.shape[1] - LINES - blocks * hours
    counts = [jnp.int32(0)] * owned
    for b in range(blocks):
        for r in range(LIST):
            code = notes_ref[b, r] - 1
            live = (code >= 0).astype(jnp.int32)
            code = jnp.maximum(code, 0)
            block = lax.rem(code, owned)
            entry = (code // owned * blocks + b) * LIST + r
            for t in range(owned):
                order[t, counts[t]] = entry
                counts[t] += live * (block == t).astype(jnp.int32)
    for t in range(owned):
        counts_ref[t] = counts[t]
        counts_ref[owned + t] = far_counts_ref[t]
    most = functools.reduce(jnp.maximum, counts)
    full = (most + GROUP - 1) // GROUP * GROUP

    for t in range(owned):

        @pl.loop(0, counts[t])
        def _(p, t=t):
            entry = order[t, p]
            r = lax.rem(entry, LIST)
            pair = entry // LIST
            dev = pair // blocks
            b = lax.rem(pair, blocks)
            g, at = p // GROUP, pl.multiple_of(lax.rem(p, GROUP) * TILE, TILE)
            for q in range(devices // blocks):
                rows = lists_ref[(q * blocks + b) * (LIST + 1) + r]
                tiles[t, g, pl.ds(at + q * piece, piece), :] = rows
            act_row = pl.multiple_of(act_rows + b * hours, 8)
            acts[t, g, :, pl.ds(at, TILE)] = activity_rows(packets_ref[dev, pl.ds(act_row, hours), :])

        @pl.loop(counts[t], full)
        def _(p, t=t):
            g, at = p // GROUP, pl.multiple_of(lax.rem(p, GROUP) * TILE, TILE)
            tiles[t, g, pl.ds(at, TILE), :] = jnp.zeros((TILE, TILE), jnp.bfloat16)
            acts[t, g, :, pl.ds(at, TILE)] = jnp.zeros((ACT, TILE), jnp.bfloat16)


def local_usage(owned, lam, counts_ref, tiles, acts, far_tiles, far_acts, near, sem):
    hours = lam.shape[0]
    hour = lax.broadcasted_iota(jnp.int32, (ACT - hours, TILE), 0)
    half = jnp.where(hour == 0, 0.5, 0.0).astype(jnp.bfloat16)
    weights = []
    for t in range(owned):
        rounded = lam[:, t * TILE : (t + 1) * TILE].astype(jnp.bfloat16)
        weights.append(jnp.concatenate([rounded * jnp.bfloat16(-0.5), half], axis=0))
    most = functools.reduce(jnp.maximum, [counts_ref[t] for t in range(owned)])

    def used(t, tile, act):
        part = lax.dot_general(
            act, weights[t], (((0,), (0,)), ((), ())), preferred_element_type=jnp.float32
        )
        share = jnp.clip(tile.astype(jnp.float32) + part, 0.0, 1.0).astype(jnp.bfloat16)
        return jnp.dot(act, share, preferred_element_type=jnp.float32)

    def group(g, totals):
        return tuple(totals[t] + used(t, tiles[t, g], acts[t, g]) for t in range(owned))

    def further(t, p, total):
        copied(far_tiles.at[t, p], near.at[:TILE], sem)
        copied(far_acts.at[t, p], near.at[TILE:], sem)
        return total + used(t, near[:TILE], near[TILE:])

    zeros = tuple(jnp.zeros((ACT, TILE), jnp.float32) for _ in range(owned))
    totals = lax.fori_loop(0, (most + GROUP - 1) // GROUP, group, zeros)
    totals = [
        lax.fori_loop(0, counts_ref[owned + t], functools.partial(further, t), totals[t])
        for t in range(owned)
    ]
    return jnp.concatenate([total[:hours] for total in totals], axis=1)


def scale_of(parts_ref, entries):
    squares = jnp.sum(jnp.sum(parts_ref[:, 0, :], axis=0, keepdims=True), axis=1, keepdims=True)
    return lax.rsqrt(squares / entries + 1e-06)


def moved(lam, gap, scale):
    return jnp.maximum(lam + 0.3 * (gap * scale), 0.0)


def direction_kernel(owned, blocks, entries, kind, *refs):
    if kind == "first":
        far, (notes_ref, far_counts_ref, packets_ref, lists_ref, limit_ref, lam_ref) = refs[:2], refs[2:8]
        gap_ref, parts_ref, counts_ref = refs[8:11]
        store = refs[11:13]
        near, sem, order = refs[13:]
        at = lam_ref[...]
        collect(
            at.shape[0], owned, blocks, notes_ref, far_counts_ref, packets_ref, lists_ref, counts_ref, *store, order
        )
    else:
        far, counts_ref, store, limit_ref = refs[:2], refs[2], refs[3:5], refs[5]
        near, sem = refs[-2:]
        refs = refs[6:-2]
        if kind == "middle":
            lam_ref, before_ref, sums_ref, gap_ref, parts_ref = refs
            at = moved(lam_ref[...], before_ref[...], scale_of(sums_ref, entries))
        else:
            anchor_ref, lam_ref, before_ref, sums_ref, gap_ref, parts_ref, lam_out_ref = refs
            extra = moved(lam_ref[...], before_ref[...], scale_of(sums_ref, entries))
            weight = 1.0 / (kind + 2.0)
            at = weight * anchor_ref[...] + (1.0 - weight) * extra
            lam_out_ref[...] = at
    gap = local_usage(owned, at, counts_ref, *store, *far, near, sem) - limit_ref[...]
    gap_ref[...] = gap
    squares = gap * gap
    line = sum(squares[:, t * TILE : (t + 1) * TILE] for t in range(owned))
    line = jnp.sum(line, axis=0, keepdims=True)
    parts_ref[...] = jnp.broadcast_to(line[None], parts_ref.shape)


def fold_kernel(parts_ref, out_ref):
    line = jnp.sum(parts_ref[:, 0, :], axis=0, keepdims=True)
    out_ref[...] = jnp.broadcast_to(line[None], out_ref.shape)


def final_kernel(entries, step, anchor_ref, lam_ref, gap_ref, sums_ref, new_ref, dir_ref):
    scale = scale_of(sums_ref, entries)
    gap = gap_ref[...]
    dir_ref[...] = gap * scale
    extra = moved(lam_ref[...], gap, scale)
    weight = 1.0 / (step + 2.0)
    new_ref[...] = weight * anchor_ref[...] + (1.0 - weight) * extra


def swapped(parts, axis):
    return lax.all_to_all(parts, axis, split_axis=0, concat_axis=0, tiled=True)


def kernel_call(body, name, out_shape, in_specs, out_specs, scratch_shapes=()):
    return pl.pallas_call(
        body,
        out_shape=out_shape,
        in_specs=in_specs,
        out_specs=out_specs,
        scratch_shapes=scratch_shapes,
        compiler_params=PARAMS,
        name=name,
    )


def on_device(scores, elig_ids, elig_counts, activity, prices, spend_limit):
    devices = lax.axis_size(USERS)
    groups = lax.axis_size("camps")
    entries = float(prices.size * devices * groups)
    hours, width = prices.shape
    owned = width // TILE
    blocks, slots = scores.shape[0], scores.shape[2]
    piece = TILE * blocks // devices
    act_rows = slots * piece
    lines = act_rows + blocks * hours
    bf16, f32, i32 = jnp.bfloat16, jnp.float32, jnp.int32
    shape = jax.ShapeDtypeStruct

    slot_ids = jnp.arange(slots, dtype=i32)
    ids = jnp.where(slot_ids[None, :] < elig_counts, elig_ids[:, 0], -1).astype(bf16)
    ids = jnp.pad(ids, ((0, LINES - blocks), (0, TILE - slots)), constant_values=-1)
    packets = kernel_call(
        cut_kernel,
        "cut",
        shape((devices, lines + LINES, TILE), bf16),
        [VMEM, HBM, HBM],
        VMEM,
        [
            pltpu.VMEM(scores.shape, bf16),
            pltpu.VMEM(activity.shape, bf16),
            pltpu.SemaphoreType.DMA((2,)),
        ],
    )(ids, scores, activity)
    packets = swapped(packets, USERS)

    which = lax.rem(lax.axis_index(USERS), blocks).astype(i32).reshape(1)
    far_slots = devices * blocks
    listed, longest, far_tiles, far_acts = kernel_call(
        functools.partial(route_kernel, owned, slots),
        "route",
        [
            shape((devices * (LIST + 1), piece, TILE), bf16),
            shape((1,), i32),
            shape((owned, far_slots, TILE, TILE), bf16),
            shape((owned, far_slots, ACT, TILE), bf16),
        ],
        [SMEM] + [VMEM] * (blocks + 1),
        [VMEM, SMEM, HBM, HBM],
        [
            pltpu.VMEM((devices, TILE), i32),
            pltpu.SMEM((devices, TILE), i32),
            pltpu.SemaphoreType.DMA,
        ],
    )(which, *(packets[:, lines + b].astype(i32) for b in range(blocks)), packets)
    near = pltpu.VMEM((TILE + ACT, TILE), bf16)

    def direct(carry):
        rows = blocks * owned * TILE + blocks * hours
        dense = kernel_call(
            functools.partial(pack_kernel, owned),
            "pack",
            shape((devices, rows + LINES, TILE), bf16),
            [SMEM, SMEM, VMEM, VMEM],
            VMEM,
        )(elig_ids, elig_counts[:, 0], scores, activity)
        dense = swapped(dense, USERS)
        flags = dense[:, rows, : blocks * owned].astype(i32)
        kept = kernel_call(
            functools.partial(far_kernel, hours, owned, blocks),
            "far",
            [shape(far_tiles.shape, bf16), shape(far_acts.shape, bf16), shape((owned,), i32)],
            [SMEM, VMEM],
            [HBM, HBM, SMEM],
            [near, pltpu.SemaphoreType.DMA],
        )(flags, dense)
        return (jnp.int32(0), *kept)

    _, far_tiles, far_acts, far_counts = lax.while_loop(
        lambda carry: carry[0] > LIST, direct, (longest[0], far_tiles, far_acts, jnp.zeros((owned,), i32))
    )
    far = (far_tiles, far_acts)
    listed = swapped(listed, USERS)
    notes = listed.reshape(devices, LIST + 1, piece, TILE)[:blocks, LIST, 0, :LIST].astype(i32)

    value = shape(prices.shape, f32)
    parts = shape((devices, 1, TILE), f32)
    scratch = [near, pltpu.SemaphoreType.DMA]
    full = pl.cdiv(blocks * LIST, GROUP)
    store_shapes = [
        shape((owned, full, GROUP * TILE, TILE), bf16),
        shape((owned, full, ACT, GROUP * TILE), bf16),
    ]

    def total_of(part):
        folded = kernel_call(fold_kernel, "fold", shape((groups, 1, TILE), f32), [VMEM], VMEM)(swapped(part, USERS))
        return swapped(folded, "camps")

    def body_of(kind):
        return functools.partial(direction_kernel, owned, blocks, entries, kind)

    got = kernel_call(
        body_of("first"),
        "direction",
        [value, parts, shape((2 * owned,), i32)] + store_shapes,
        [HBM, HBM, SMEM, SMEM] + [VMEM] * 4,
        [VMEM, VMEM, SMEM, VMEM, VMEM],
        scratch + [pltpu.SMEM((owned, blocks * LIST), i32)],
    )(*far, notes, far_counts, packets, listed, spend_limit, prices)
    gap, sums, kept = got[0], total_of(got[1]), got[2:]

    def direction(kind, *args):
        outs = [value, parts] + ([value] if kind != "middle" else [])
        got = kernel_call(
            body_of(kind),
            "direction",
            outs,
            [HBM, HBM, SMEM] + [VMEM] * (len(args) + 3),
            [VMEM] * len(outs),
            scratch,
        )(*far, *kept, spend_limit, *args)
        return got[0], total_of(got[1]), got[2:]

    lam = prices
    for step in range(STEPS):
        gap, sums, _ = direction("middle", lam, gap, sums)
        if step < STEPS - 1:
            gap, sums, (lam,) = direction(step, prices, lam, gap, sums)
    new, last = kernel_call(
        functools.partial(final_kernel, entries, STEPS - 1), "final", [value, value], [VMEM] * 4, [VMEM] * 2
    )(prices, lam, gap, sums)
    return (new, last)


def solution(mesh):
    torus = Mesh(
        mesh.devices.reshape(4, 4, 2, mesh.shape["camps"]),
        ("users_0", "users_1", "users_2", "camps"),
    )
    in_specs = (
        P(USERS, "camps", None, None, None),
        P(USERS, "camps", None),
        P(USERS, "camps"),
        P(None, USERS),
        P(None, USERS_CAMPS),
        P(None, USERS_CAMPS),
    )
    out_specs = (P(None, USERS_CAMPS), P(None, USERS_CAMPS))
    return jax.shard_map(
        on_device, mesh=torus, in_specs=in_specs, out_specs=out_specs, check_vma=False
    )
```

```python
import functools

import jax
import jax.numpy as jnp
from jax import lax
from jax.experimental import pallas as pl
from jax.experimental.pallas import tpu as pltpu
from jax.sharding import Mesh
from jax.sharding import PartitionSpec as P

STEPS = 2
USERS = ("users_0", "users_1", "users_2")
USERS_CAMPS = ("users_0", "users_1", "users_2", "camps")
TILE = 128
LINES = 8
ACT = 32
UNROLL = 4
SUM_LANE = 64

VMEM = pl.BlockSpec(memory_space=pltpu.VMEM)
HBM = pl.BlockSpec(memory_space=pltpu.HBM)
PARAMS = pltpu.CompilerParams(vmem_limit_bytes=8 * 2**20)
NT = (((1,), (1,)), ((), ()))


def rounded(value):
    return value.astype(jnp.bfloat16).astype(jnp.float32)


def cut_kernel(ids_ref, prices_ref, limit_ref, scores_hbm, act_hbm, out_ref, scores, act, sems):
    load_act = pltpu.make_async_copy(act_hbm, act, sems.at[0])
    load_scores = pltpu.make_async_copy(scores_hbm, scores, sems.at[1])
    load_act.start()
    load_scores.start()
    devices = out_ref.shape[0]
    hours, campaigns = prices_ref.shape
    blocks, slots = scores.shape[0], scores.shape[2]
    owned = campaigns // TILE
    w = TILE // devices
    span = owned * w
    acts = blocks * slots * w
    values = acts + blocks * hours
    lines = values + span
    row = lax.broadcasted_iota(jnp.int32, (campaigns, campaigns), 0)
    col = lax.broadcasted_iota(jnp.int32, (campaigns, campaigns), 1)
    source = lax.rem(row, span) // w * TILE + row // span * w + lax.rem(row, w)
    pick = jnp.where(col == source, 1.0, 0.0)
    pick_half = (pick * 0.5).astype(jnp.bfloat16)
    pick = pick.astype(jnp.bfloat16)

    price, limit = prices_ref[...], limit_ref[...]
    high = rounded(price)
    middle = rounded(price - high)
    limit_high = rounded(limit)
    terms = [high, middle, price - high - middle, limit_high, limit - limit_high]
    terms.append(jnp.zeros((TILE - len(terms) * hours, campaigns), jnp.float32))
    terms = jnp.concatenate(terms, axis=0).astype(jnp.bfloat16)
    terms = lax.dot_general(pick, terms, NT, preferred_element_type=jnp.float32).astype(jnp.bfloat16)
    ids = ids_ref[...]
    for m in range(devices):
        out_ref[m, values : values + span, :] = terms[m * span : (m + 1) * span]
        out_ref[m, lines : lines + LINES, :] = ids
    load_act.wait()
    for b in range(blocks):
        own = act[:, b * TILE : (b + 1) * TILE]
        for m in range(devices):
            out_ref[m, acts + b * hours : acts + (b + 1) * hours, :] = own
    load_scores.wait()
    for b in range(blocks):
        for k in range(0, slots, owned):
            tiles = jnp.concatenate([scores[b, 0, k + j] for j in range(owned)], axis=1)
            cut = lax.dot_general(pick_half, tiles, NT, preferred_element_type=jnp.float32).astype(jnp.bfloat16)
            at = (b * slots + k) * w
            for m in range(devices):
                out_ref[m, at : at + span, :] = cut[m * span : (m + 1) * span]


def unpack(hours, blocks, rows, packets_ref, anchor_ref, limit_ref, hot_ref, acts_ref):
    devices = packets_ref.shape[0]
    campaigns = anchor_ref.shape[1]
    span = campaigns // devices
    w = TILE // devices
    act_row = blocks * rows
    values = act_row + blocks * hours
    lines = values + span
    terms = packets_ref[:, values : values + span, :].reshape(campaigns, TILE).astype(jnp.float32).T
    terms = [terms[n * hours : (n + 1) * hours] for n in range(5)]
    anchor_ref[...] = terms[0] + terms[1] + terms[2]
    limit_ref[...] = terms[3] + terms[4]
    hour = lax.broadcasted_iota(jnp.int32, (ACT - hours, TILE), 0)
    tail = jnp.where(hour == 0, 1.0, 0.0).astype(jnp.bfloat16)
    slot = lax.broadcasted_iota(jnp.int32, (rows, TILE), 0) // w
    own_slot = slot == lax.broadcasted_iota(jnp.int32, (rows, TILE), 1)
    column = lax.rem(lax.broadcasted_iota(jnp.int32, (rows, campaigns), 0), w)
    wanted = (lax.broadcasted_iota(jnp.int32, (rows, campaigns), 1) - column).astype(jnp.float32)
    ones = jnp.ones((TILE, campaigns), jnp.bfloat16)

    @pl.loop(0, devices // UNROLL)
    def _(step):
        for n in range(UNROLL):
            i = step * UNROLL + n
            ids = packets_ref[i, lines : lines + LINES, :].astype(jnp.float32)
            for b in range(blocks):
                spread = jnp.where(own_slot, ids[b : b + 1, :], 0.0).astype(jnp.bfloat16)
                first = jnp.dot(spread, ones, preferred_element_type=jnp.float32)
                hot_ref[i, b * rows : (b + 1) * rows, :] = jnp.where(first == wanted, 1.0, 0.0).astype(jnp.bfloat16)
                acts_ref[i, b * ACT : b * ACT + hours, :] = packets_ref[i, act_row + b * hours : act_row + (b + 1) * hours, :]
                acts_ref[i, b * ACT + hours : (b + 1) * ACT, :] = tail


def usage_at(lam, blocks, rows, packets_ref, hot_ref, acts_ref):
    hours, campaigns = lam.shape
    devices = packets_ref.shape[0]
    hour = lax.broadcasted_iota(jnp.int32, (ACT - hours, campaigns), 0)
    half = jnp.where(hour == 0, 0.5, 0.0)
    table = jnp.concatenate([rounded(lam) * -0.5, half], axis=0).astype(jnp.bfloat16)

    def senders(step, total):
        for n in range(UNROLL):
            i = step * UNROLL + n
            named = lax.dot_general(
                hot_ref[i], table, NT, preferred_element_type=jnp.float32
            ).astype(jnp.bfloat16)
            for b in range(blocks):
                act = acts_ref[i, b * ACT : (b + 1) * ACT, :]
                part = jnp.dot(named[b * rows : (b + 1) * rows], act, preferred_element_type=jnp.float32)
                score = packets_ref[i, b * rows : (b + 1) * rows, :].astype(jnp.float32)
                share = jnp.clip(score + part, 0.0, 1.0).astype(jnp.bfloat16)
                used = lax.dot_general(act, share, NT, preferred_element_type=jnp.float32)
                high = rounded(used)
                both = jnp.concatenate([high, used - high], axis=0).astype(jnp.bfloat16)
                hot = hot_ref[i, b * rows : (b + 1) * rows, :]
                total = total + jnp.dot(both, hot, preferred_element_type=jnp.float32)
        return total

    total = lax.fori_loop(0, devices // UNROLL, senders, jnp.zeros((2 * ACT, campaigns), jnp.float32))
    return total[:hours] + total[ACT : ACT + hours]


def scale_of(parts_ref, entries):
    squares = jnp.sum(jnp.sum(parts_ref[:, 0, :], axis=0, keepdims=True), axis=1, keepdims=True)
    return lax.rsqrt(squares / entries + 1e-06)


def moved(lam, gap, scale):
    return jnp.maximum(lam + 0.3 * (gap * scale), 0.0)


def direction_kernel(blocks, rows, entries, kind, *refs):
    if kind == "first":
        packets_ref, gap_ref, send_ref, anchor_ref, limit_ref, hot_ref, acts_ref = refs
        hours = gap_ref.shape[0]
        unpack(hours, blocks, rows, packets_ref, anchor_ref, limit_ref, hot_ref, acts_ref)
        at = anchor_ref[...]
    elif kind == "middle":
        packets_ref, anchor_ref, limit_ref, hot_ref, acts_ref, before_ref, sums_ref, gap_ref, send_ref = refs
        at = moved(anchor_ref[...], before_ref[...], scale_of(sums_ref, entries))
    elif kind == "last":
        packets_ref, anchor_ref, limit_ref, hot_ref, acts_ref, lam_ref, before_ref, sums_ref, send_ref = refs
        at = moved(lam_ref[...], before_ref[...], scale_of(sums_ref, entries))
    else:
        packets_ref, anchor_ref, limit_ref, hot_ref, acts_ref = refs[:5]
        lam_ref, before_ref, sums_ref, gap_ref, send_ref, lam_out_ref = refs[5:]
        extra = moved(lam_ref[...], before_ref[...], scale_of(sums_ref, entries))
        weight = 1.0 / (kind + 2.0)
        at = weight * anchor_ref[...] + (1.0 - weight) * extra
        lam_out_ref[...] = at
    gap = usage_at(at, blocks, rows, packets_ref, hot_ref, acts_ref) - limit_ref[...]
    line = jnp.sum(gap * gap, axis=0, keepdims=True)
    if kind != "last":
        gap_ref[...] = gap
        line = sum(line[:, n : n + TILE] for n in range(0, line.shape[1], TILE))
        send_ref[...] = jnp.broadcast_to(line[None], send_ref.shape)
        return
    hours, campaigns = gap.shape
    devices, span = send_ref.shape[:2]
    squares = jnp.broadcast_to(jnp.sum(line, axis=1, keepdims=True), (LINES, campaigns))
    results = [gap, lam_ref[...]]
    results.append(jnp.zeros((SUM_LANE - 2 * hours, campaigns), jnp.float32))
    results.append(squares)
    results.append(jnp.zeros((TILE - SUM_LANE - LINES, campaigns), jnp.float32))
    results = jnp.concatenate(results, axis=0).T
    for i in range(devices):
        send_ref[i] = results[i * span : (i + 1) * span]


def fold_kernel(last, parts_ref, out_ref):
    line = jnp.sum(parts_ref[:, 0, :], axis=0, keepdims=True)
    if last:
        lane = lax.broadcasted_iota(jnp.int32, line.shape, 1)
        line = jnp.where(lane == SUM_LANE, line, 0.0)
    out_ref[...] = jnp.broadcast_to(line[None], out_ref.shape)


def final_kernel(entries, step, anchor_ref, parts_ref, sums_ref, new_ref, dir_ref, rows):
    devices, span = parts_ref.shape[:2]
    hours, campaigns = anchor_ref.shape
    w = TILE // devices
    for m in range(devices):
        for j in range(span // w):
            rows[j * TILE + m * w : j * TILE + (m + 1) * w, :] = parts_ref[m, j * w : (j + 1) * w, :]
    results = rows[...].T
    gap, lam = results[:hours], results[hours : 2 * hours]
    scale = scale_of(sums_ref, entries)
    dir_ref[...] = gap * scale
    weight = 1.0 / (step + 2.0)
    new_ref[...] = weight * anchor_ref[...] + (1.0 - weight) * moved(lam, gap, scale)


def swapped(parts, axis):
    return lax.all_to_all(parts, axis, split_axis=0, concat_axis=0, tiled=True)


def kernel_call(body, name, out_shape, in_specs, out_specs, scratch_shapes=()):
    return pl.pallas_call(
        body,
        out_shape=out_shape,
        in_specs=in_specs,
        out_specs=out_specs,
        scratch_shapes=scratch_shapes,
        compiler_params=PARAMS,
        name=name,
    )


def on_device(scores, elig_ids, elig_counts, activity, prices, spend_limit):
    devices = lax.axis_size(USERS)
    groups = lax.axis_size("camps")
    entries = float(prices.size * devices * groups)
    hours, campaigns = prices.shape
    blocks, slots = scores.shape[0], scores.shape[2]
    w = TILE // devices
    span = campaigns // TILE * w
    rows = slots * w
    bf16, f32, i32 = jnp.bfloat16, jnp.float32, jnp.int32
    shape = jax.ShapeDtypeStruct

    slot_ids = jnp.arange(slots, dtype=i32)
    ids = jnp.where(slot_ids[None, :] < elig_counts, elig_ids[:, 0] * w, -TILE).astype(bf16)
    ids = jnp.pad(ids, ((0, LINES - blocks), (0, TILE - slots)))
    packets = kernel_call(
        cut_kernel,
        "cut",
        shape((devices, blocks * (rows + hours) + span + LINES, TILE), bf16),
        [VMEM, VMEM, VMEM, HBM, HBM],
        VMEM,
        [
            pltpu.VMEM(scores.shape, bf16),
            pltpu.VMEM(activity.shape, bf16),
            pltpu.SemaphoreType.DMA((2,)),
        ],
    )(ids, prices, spend_limit, scores, activity)
    packets = swapped(packets, USERS)

    value = shape(prices.shape, f32)
    part = shape((devices, 1, TILE), f32)

    def total_of(parts, last=False):
        folded = kernel_call(
            functools.partial(fold_kernel, last), "fold", shape((groups, 1, TILE), f32), [VMEM], VMEM
        )(parts)
        return swapped(folded, "camps")

    def direction(kind, outs, *args):
        return kernel_call(
            functools.partial(direction_kernel, blocks, rows, entries, kind),
            "direction",
            outs,
            [VMEM] * len(args),
            [VMEM] * len(outs),
        )(*args)

    kept_shapes = [
        value,
        value,
        shape((devices, blocks * rows, campaigns), bf16),
        shape((devices, blocks * ACT, TILE), bf16),
    ]
    gap, parts, *kept = direction("first", [value, part] + kept_shapes, packets)
    lam = kept[0]
    for step in range(STEPS - 1):
        sums = total_of(swapped(parts, USERS))
        gap, parts = direction("middle", [value, part], packets, *kept, gap, sums)
        sums = total_of(swapped(parts, USERS))
        gap, parts, lam = direction(step, [value, part, value], packets, *kept, lam, gap, sums)
    sums = total_of(swapped(parts, USERS))
    (parts,) = direction("last", [shape((devices, span, TILE), f32)], packets, *kept, lam, gap, sums)
    parts = swapped(parts, USERS)
    new, last = kernel_call(
        functools.partial(final_kernel, entries, STEPS - 1),
        "final",
        [value, value],
        [VMEM] * 3,
        [VMEM] * 2,
        [pltpu.VMEM((campaigns, TILE), f32)],
    )(prices, parts, total_of(parts, last=True))
    return (new, last)


def solution(mesh):
    torus = Mesh(
        mesh.devices.reshape(4, 4, 2, mesh.shape["camps"]),
        ("users_0", "users_1", "users_2", "camps"),
    )
    in_specs = (
        P(USERS, "camps", None, None, None),
        P(USERS, "camps", None),
        P(USERS, "camps"),
        P(None, USERS),
        P(None, USERS_CAMPS),
        P(None, USERS_CAMPS),
    )
    out_specs = (P(None, USERS_CAMPS), P(None, USERS_CAMPS))
    return jax.shard_map(
        on_device, mesh=torus, in_specs=in_specs, out_specs=out_specs, check_vma=False
    )
```

```python
import functools

import jax
import jax.numpy as jnp
from jax import lax
from jax.experimental import pallas as pl
from jax.experimental.pallas import tpu as pltpu
from jax.sharding import Mesh
from jax.sharding import PartitionSpec as P

STEPS = 2
USERS = ("users_0", "users_1", "users_2")
USERS_CAMPS = ("users_0", "users_1", "users_2", "camps")
TILE = 128
LINES = 8
ACT = 32
CHUNK = 16
UNROLL = 8
SUM_LANE = 64

VMEM = pl.BlockSpec(memory_space=pltpu.VMEM)
HBM = pl.BlockSpec(memory_space=pltpu.HBM)
PARAMS = pltpu.CompilerParams(vmem_limit_bytes=8 * 2**20)
NT = (((1,), (1,)), ((), ()))


def rounded(value):
    return value.astype(jnp.bfloat16).astype(jnp.float32)


def cut_kernel(ids_ref, prices_ref, limit_ref, scores_hbm, act_hbm, out_ref, scores, act, sems):
    load_act = pltpu.make_async_copy(act_hbm, act, sems.at[0])
    load_scores = pltpu.make_async_copy(scores_hbm, scores, sems.at[1])
    load_act.start()
    load_scores.start()
    devices = out_ref.shape[0]
    hours, campaigns = prices_ref.shape
    blocks, slots = scores.shape[0], scores.shape[2]
    owned = campaigns // TILE
    w = TILE // devices
    span = owned * w
    acts = blocks * slots * w
    values = acts + blocks * hours
    lines = values + span
    row = lax.broadcasted_iota(jnp.int32, (campaigns, campaigns), 0)
    col = lax.broadcasted_iota(jnp.int32, (campaigns, campaigns), 1)
    source = lax.rem(row, span) // w * TILE + row // span * w + lax.rem(row, w)
    pick = jnp.where(col == source, 1.0, 0.0)
    pick_half = (pick * 0.5).astype(jnp.bfloat16)
    pick = pick.astype(jnp.bfloat16)

    price, limit = prices_ref[...], limit_ref[...]
    high = rounded(price)
    middle = rounded(price - high)
    limit_high = rounded(limit)
    terms = [high, middle, price - high - middle, limit_high, limit - limit_high]
    terms.append(jnp.zeros((TILE - len(terms) * hours, campaigns), jnp.float32))
    terms = jnp.concatenate(terms, axis=0).astype(jnp.bfloat16)
    terms = lax.dot_general(pick, terms, NT, preferred_element_type=jnp.float32).astype(jnp.bfloat16)
    ids = ids_ref[...]
    for m in range(devices):
        out_ref[m, values : values + span, :] = terms[m * span : (m + 1) * span]
        out_ref[m, lines : lines + LINES, :] = ids
    load_act.wait()
    for b in range(blocks):
        own = act[:, b * TILE : (b + 1) * TILE]
        for m in range(devices):
            out_ref[m, acts + b * hours : acts + (b + 1) * hours, :] = own
    load_scores.wait()
    for b in range(blocks):
        for k in range(0, slots, owned):
            tiles = jnp.concatenate([scores[b, 0, k + j] for j in range(owned)], axis=1)
            cut = lax.dot_general(pick_half, tiles, NT, preferred_element_type=jnp.float32).astype(jnp.bfloat16)
            at = (b * slots + k) * w
            for m in range(devices):
                out_ref[m, at : at + span, :] = cut[m * span : (m + 1) * span]


def unpack(hours, blocks, rows, packets_ref, anchor_ref, limit_ref, hot_ref, acts_ref):
    devices = packets_ref.shape[0]
    campaigns = anchor_ref.shape[1]
    span = campaigns // devices
    w = TILE // devices
    act_row = blocks * rows
    values = act_row + blocks * hours
    lines = values + span
    terms = packets_ref[:, values : values + span, :].reshape(campaigns, TILE).astype(jnp.float32).T
    terms = [terms[n * hours : (n + 1) * hours] for n in range(5)]
    anchor_ref[...] = terms[0] + terms[1] + terms[2]
    limit_ref[...] = terms[3] + terms[4]
    hour = lax.broadcasted_iota(jnp.int32, (ACT - hours, TILE), 0)
    tail = jnp.where(hour == 0, 1.0, 0.0).astype(jnp.bfloat16)
    padded = hot_ref.shape[1]
    row = lax.broadcasted_iota(jnp.int32, (padded, TILE), 0)
    own_slot = lax.rem(row, rows) // w == lax.broadcasted_iota(jnp.int32, (padded, TILE), 1)
    row_block = row // rows
    row = lax.broadcasted_iota(jnp.int32, (padded, campaigns), 0)
    wanted = lax.broadcasted_iota(jnp.int32, (padded, campaigns), 1) - lax.rem(row, w)
    wanted = jnp.where(row < blocks * rows, wanted, -2 * TILE).astype(jnp.float32)
    ones = jnp.ones((TILE, campaigns), jnp.bfloat16)

    @pl.loop(0, devices // UNROLL)
    def _(step):
        for n in range(UNROLL):
            i = step * UNROLL + n
            ids = packets_ref[i, lines : lines + LINES, :].astype(jnp.float32)
            spread = jnp.zeros((padded, TILE), jnp.float32)
            for b in range(blocks):
                mine = jnp.logical_and(own_slot, row_block == b)
                spread = jnp.where(mine, ids[b : b + 1, :], spread)
                acts_ref[i, b * ACT : b * ACT + hours, :] = packets_ref[i, act_row + b * hours : act_row + (b + 1) * hours, :]
                acts_ref[i, b * ACT + hours : (b + 1) * ACT, :] = tail
            first = jnp.dot(spread.astype(jnp.bfloat16), ones, preferred_element_type=jnp.float32)
            hot_ref[i] = jnp.where(first == wanted, 1.0, 0.0).astype(jnp.bfloat16)


def usage_at(lam, blocks, rows, packets_ref, hot_ref, acts_ref, named_ref, share_ref, used_ref):
    hours, campaigns = lam.shape
    devices, padded = hot_ref.shape[:2]
    chunk = share_ref.shape[0]
    listed = blocks * rows
    hour = lax.broadcasted_iota(jnp.int32, (ACT - hours, campaigns), 0)
    half = jnp.where(hour == 0, 0.5, 0.0)
    table = jnp.concatenate([rounded(lam) * -0.5, half] * blocks, axis=0).astype(jnp.bfloat16)
    row = lax.broadcasted_iota(jnp.int32, (padded, blocks * ACT), 0)
    own = row // rows == lax.broadcasted_iota(jnp.int32, (padded, blocks * ACT), 1) // ACT
    block = lax.broadcasted_iota(jnp.int32, (ACT, padded), 1) // rows
    if listed < padded:
        share_ref[:, listed:, :] = jnp.zeros((chunk, padded - listed, TILE), jnp.bfloat16)

    def senders(step, total):
        first = step * chunk
        hot = [hot_ref[first + n] for n in range(chunk)]
        for n in range(chunk):
            named = lax.dot_general(hot[n], table, NT, preferred_element_type=jnp.float32)
            named_ref[n] = jnp.where(own, named, 0.0).astype(jnp.bfloat16)
        for n in range(chunk):
            part = jnp.dot(named_ref[n, :listed, :], acts_ref[first + n], preferred_element_type=jnp.float32)
            score = packets_ref[first + n, :listed, :].astype(jnp.float32)
            share_ref[n, :listed, :] = jnp.clip(score + part, 0.0, 1.0).astype(jnp.bfloat16)
        for n in range(chunk):
            each = lax.dot_general(acts_ref[first + n], share_ref[n], NT, preferred_element_type=jnp.float32)
            used = each[:ACT]
            for b in range(1, blocks):
                used = jnp.where(block == b, each[b * ACT : (b + 1) * ACT], used)
            high = rounded(used)
            both = jnp.concatenate([high, used - high], axis=0).astype(jnp.bfloat16)
            used_ref[:, n * padded : (n + 1) * padded] = both
        hot = hot_ref[pl.ds(first, chunk)].reshape(chunk * padded, campaigns)
        return total + jnp.dot(used_ref[...], hot, preferred_element_type=jnp.float32)

    total = jnp.zeros((2 * ACT, campaigns), jnp.float32)
    total = lax.fori_loop(0, devices // chunk, senders, total)
    return total[:hours] + total[ACT : ACT + hours]


def scale_of(parts_ref, entries):
    squares = jnp.sum(jnp.sum(parts_ref[:, 0, :], axis=0, keepdims=True), axis=1, keepdims=True)
    return lax.rsqrt(squares / entries + 1e-06)


def moved(lam, gap, scale):
    return jnp.maximum(lam + 0.3 * (gap * scale), 0.0)


def direction_kernel(blocks, rows, entries, kind, *refs):
    refs, scratch = refs[:-3], refs[-3:]
    if kind == "first":
        packets_ref, gap_ref, send_ref, anchor_ref, limit_ref, hot_ref, acts_ref = refs
        hours = gap_ref.shape[0]
        unpack(hours, blocks, rows, packets_ref, anchor_ref, limit_ref, hot_ref, acts_ref)
        at = anchor_ref[...]
    elif kind == "middle":
        packets_ref, anchor_ref, limit_ref, hot_ref, acts_ref, before_ref, sums_ref, gap_ref, send_ref = refs
        at = moved(anchor_ref[...], before_ref[...], scale_of(sums_ref, entries))
    elif kind == "last":
        packets_ref, anchor_ref, limit_ref, hot_ref, acts_ref, lam_ref, before_ref, sums_ref, send_ref = refs
        at = moved(lam_ref[...], before_ref[...], scale_of(sums_ref, entries))
    else:
        packets_ref, anchor_ref, limit_ref, hot_ref, acts_ref = refs[:5]
        lam_ref, before_ref, sums_ref, gap_ref, send_ref, lam_out_ref = refs[5:]
        extra = moved(lam_ref[...], before_ref[...], scale_of(sums_ref, entries))
        weight = 1.0 / (kind + 2.0)
        at = weight * anchor_ref[...] + (1.0 - weight) * extra
        lam_out_ref[...] = at
    gap = usage_at(at, blocks, rows, packets_ref, hot_ref, acts_ref, *scratch) - limit_ref[...]
    line = jnp.sum(gap * gap, axis=0, keepdims=True)
    if kind != "last":
        gap_ref[...] = gap
        line = sum(line[:, n : n + TILE] for n in range(0, line.shape[1], TILE))
        send_ref[...] = jnp.broadcast_to(line[None], send_ref.shape)
        return
    hours, campaigns = gap.shape
    devices, span = send_ref.shape[:2]
    squares = jnp.broadcast_to(jnp.sum(line, axis=1, keepdims=True), (LINES, campaigns))
    results = [gap, lam_ref[...]]
    results.append(jnp.zeros((SUM_LANE - 2 * hours, campaigns), jnp.float32))
    results.append(squares)
    results.append(jnp.zeros((TILE - SUM_LANE - LINES, campaigns), jnp.float32))
    results = jnp.concatenate(results, axis=0).T
    for i in range(devices):
        send_ref[i] = results[i * span : (i + 1) * span]


def fold_kernel(last, parts_ref, out_ref):
    line = jnp.sum(parts_ref[:, 0, :], axis=0, keepdims=True)
    if last:
        lane = lax.broadcasted_iota(jnp.int32, line.shape, 1)
        line = jnp.where(lane == SUM_LANE, line, 0.0)
    out_ref[...] = jnp.broadcast_to(line[None], out_ref.shape)


def final_kernel(entries, step, anchor_ref, parts_ref, sums_ref, new_ref, dir_ref, rows):
    devices, span = parts_ref.shape[:2]
    hours, campaigns = anchor_ref.shape
    w = TILE // devices
    for m in range(devices):
        for j in range(span // w):
            rows[j * TILE + m * w : j * TILE + (m + 1) * w, :] = parts_ref[m, j * w : (j + 1) * w, :]
    results = rows[...].T
    gap, lam = results[:hours], results[hours : 2 * hours]
    scale = scale_of(sums_ref, entries)
    dir_ref[...] = gap * scale
    weight = 1.0 / (step + 2.0)
    new_ref[...] = weight * anchor_ref[...] + (1.0 - weight) * moved(lam, gap, scale)


def swapped(parts, axis):
    return lax.all_to_all(parts, axis, split_axis=0, concat_axis=0, tiled=True)


def kernel_call(body, name, out_shape, in_specs, out_specs, scratch_shapes=()):
    return pl.pallas_call(
        body,
        out_shape=out_shape,
        in_specs=in_specs,
        out_specs=out_specs,
        scratch_shapes=scratch_shapes,
        compiler_params=PARAMS,
        name=name,
    )


def on_device(scores, elig_ids, elig_counts, activity, prices, spend_limit):
    devices = lax.axis_size(USERS)
    groups = lax.axis_size("camps")
    entries = float(prices.size * devices * groups)
    hours, campaigns = prices.shape
    blocks, slots = scores.shape[0], scores.shape[2]
    w = TILE // devices
    span = campaigns // TILE * w
    rows = slots * w
    padded = pl.cdiv(blocks * rows, TILE) * TILE
    chunk = min(CHUNK, devices)
    bf16, f32, i32 = jnp.bfloat16, jnp.float32, jnp.int32
    shape = jax.ShapeDtypeStruct

    slot_ids = jnp.arange(slots, dtype=i32)
    ids = jnp.where(slot_ids[None, :] < elig_counts, elig_ids[:, 0] * w, -TILE).astype(bf16)
    ids = jnp.pad(ids, ((0, LINES - blocks), (0, TILE - slots)))
    packets = kernel_call(
        cut_kernel,
        "cut",
        shape((devices, blocks * (rows + hours) + span + LINES, TILE), bf16),
        [VMEM, VMEM, VMEM, HBM, HBM],
        VMEM,
        [
            pltpu.VMEM(scores.shape, bf16),
            pltpu.VMEM(activity.shape, bf16),
            pltpu.SemaphoreType.DMA((2,)),
        ],
    )(ids, prices, spend_limit, scores, activity)
    packets = swapped(packets, USERS)

    value = shape(prices.shape, f32)
    part = shape((devices, 1, TILE), f32)

    def total_of(parts, last=False):
        folded = kernel_call(
            functools.partial(fold_kernel, last), "fold", shape((groups, 1, TILE), f32), [VMEM], VMEM
        )(parts)
        return swapped(folded, "camps")

    def direction(kind, outs, *args):
        return kernel_call(
            functools.partial(direction_kernel, blocks, rows, entries, kind),
            "direction",
            outs,
            [VMEM] * len(args),
            [VMEM] * len(outs),
            [
                pltpu.VMEM((chunk, padded, blocks * ACT), bf16),
                pltpu.VMEM((chunk, padded, TILE), bf16),
                pltpu.VMEM((2 * ACT, chunk * padded), bf16),
            ],
        )(*args)

    kept_shapes = [
        value,
        value,
        shape((devices, padded, campaigns), bf16),
        shape((devices, blocks * ACT, TILE), bf16),
    ]
    gap, parts, *kept = direction("first", [value, part] + kept_shapes, packets)
    lam = kept[0]
    for step in range(STEPS - 1):
        sums = total_of(swapped(parts, USERS))
        gap, parts = direction("middle", [value, part], packets, *kept, gap, sums)
        sums = total_of(swapped(parts, USERS))
        gap, parts, lam = direction(step, [value, part, value], packets, *kept, lam, gap, sums)
    sums = total_of(swapped(parts, USERS))
    (parts,) = direction("last", [shape((devices, span, TILE), f32)], packets, *kept, lam, gap, sums)
    parts = swapped(parts, USERS)
    new, last = kernel_call(
        functools.partial(final_kernel, entries, STEPS - 1),
        "final",
        [value, value],
        [VMEM] * 3,
        [VMEM] * 2,
        [pltpu.VMEM((campaigns, TILE), f32)],
    )(prices, parts, total_of(parts, last=True))
    return (new, last)


def solution(mesh):
    torus = Mesh(
        mesh.devices.reshape(4, 4, 2, mesh.shape["camps"]),
        ("users_0", "users_1", "users_2", "camps"),
    )
    in_specs = (
        P(USERS, "camps", None, None, None),
        P(USERS, "camps", None),
        P(USERS, "camps"),
        P(None, USERS),
        P(None, USERS_CAMPS),
        P(None, USERS_CAMPS),
    )
    out_specs = (P(None, USERS_CAMPS), P(None, USERS_CAMPS))
    return jax.shard_map(
        on_device, mesh=torus, in_specs=in_specs, out_specs=out_specs, check_vma=False
    )
```

```python
import functools

import jax
import jax.numpy as jnp
from jax import lax
from jax.experimental import pallas as pl
from jax.experimental.pallas import tpu as pltpu
from jax.sharding import Mesh
from jax.sharding import PartitionSpec as P

STEPS = 2
USERS = ("users_0", "users_1", "users_2")
USERS_CAMPS = ("users_0", "users_1", "users_2", "camps")
TILE = 128
LINES = 8
ACT = 32
CHUNK = 32
UNROLL = 8
SUM_LANE = 64

VMEM = pl.BlockSpec(memory_space=pltpu.VMEM)
HBM = pl.BlockSpec(memory_space=pltpu.HBM)
PARAMS = pltpu.CompilerParams(vmem_limit_bytes=8 * 2**20)
NT = (((1,), (1,)), ((), ()))


def rounded(value):
    return value.astype(jnp.bfloat16).astype(jnp.float32)


def cut_kernel(scores_hbm, ids_hbm, counts_hbm, prices_hbm, limit_hbm, act_hbm, out_ref, *scratch):
    scores, ids, counts, prices, limits, act, sems = scratch
    sources = (scores_hbm, ids_hbm, counts_hbm, prices_hbm, limit_hbm, act_hbm)
    loads = [pltpu.make_async_copy(sources[n], scratch[n], sems.at[n]) for n in range(len(sources))]
    for load in loads:
        load.start()
    devices = out_ref.shape[0]
    hours, campaigns = prices.shape
    blocks, slots = scores.shape[0], scores.shape[2]
    owned = campaigns // TILE
    w = TILE // devices
    span = owned * w
    acts = blocks * slots * w
    values = acts + blocks * hours
    lines = values + span
    row = lax.broadcasted_iota(jnp.int32, (campaigns, campaigns), 0)
    col = lax.broadcasted_iota(jnp.int32, (campaigns, campaigns), 1)
    source = lax.rem(row, span) // w * TILE + row // span * w + lax.rem(row, w)
    pick = jnp.where(col == source, 1.0, 0.0)
    pick_half = (pick * 0.5).astype(jnp.bfloat16)
    pick = pick.astype(jnp.bfloat16)

    loads[3].wait()
    loads[4].wait()
    price, limit = prices[...], limits[...]
    high = rounded(price)
    middle = rounded(price - high)
    limit_high = rounded(limit)
    terms = [high, middle, price - high - middle, limit_high, limit - limit_high]
    terms.append(jnp.zeros((TILE - len(terms) * hours, campaigns), jnp.float32))
    terms = jnp.concatenate(terms, axis=0).astype(jnp.bfloat16)
    terms = lax.dot_general(pick, terms, NT, preferred_element_type=jnp.float32).astype(jnp.bfloat16)
    loads[1].wait()
    loads[2].wait()
    row = lax.broadcasted_iota(jnp.int32, (LINES, TILE), 0)
    lane = lax.broadcasted_iota(jnp.int32, (LINES, TILE), 1)
    entries = jnp.full((LINES, TILE), -TILE, jnp.int32)
    for b in range(blocks):
        for k in range(slots):
            here = jnp.logical_and(row == b, lane == k)
            entries = jnp.where(here, jnp.where(k < counts[b], ids[b, 0, k] * w, -TILE), entries)
    entries = entries.astype(jnp.float32).astype(jnp.bfloat16)
    for m in range(devices):
        out_ref[m, values : values + span, :] = terms[m * span : (m + 1) * span]
        out_ref[m, lines : lines + LINES, :] = entries
    loads[5].wait()
    for b in range(blocks):
        own = act[:, b * TILE : (b + 1) * TILE]
        for m in range(devices):
            out_ref[m, acts + b * hours : acts + (b + 1) * hours, :] = own
    loads[0].wait()
    for b in range(blocks):
        for k in range(0, slots, owned):
            tiles = jnp.concatenate([scores[b, 0, k + j] for j in range(owned)], axis=1)
            cut = lax.dot_general(pick_half, tiles, NT, preferred_element_type=jnp.float32).astype(jnp.bfloat16)
            at = (b * slots + k) * w
            for m in range(devices):
                out_ref[m, at : at + span, :] = cut[m * span : (m + 1) * span]


def unpack(hours, blocks, rows, packets_ref, anchor_ref, limit_ref, hot_ref, acts_ref):
    devices = packets_ref.shape[0]
    campaigns = anchor_ref.shape[1]
    span = campaigns // devices
    w = TILE // devices
    act_row = blocks * rows
    values = act_row + blocks * hours
    lines = values + span
    terms = packets_ref[:, values : values + span, :].reshape(campaigns, TILE).astype(jnp.float32).T
    terms = [terms[n * hours : (n + 1) * hours] for n in range(5)]
    anchor_ref[...] = terms[0] + terms[1] + terms[2]
    limit_ref[...] = terms[3] + terms[4]
    hour = lax.broadcasted_iota(jnp.int32, (ACT - hours, TILE), 0)
    tail = jnp.where(hour == 0, 1.0, 0.0).astype(jnp.bfloat16)
    padded = hot_ref.shape[1]
    row = lax.broadcasted_iota(jnp.int32, (padded, TILE), 0)
    own_slot = lax.rem(row, rows) // w == lax.broadcasted_iota(jnp.int32, (padded, TILE), 1)
    row_block = row // rows
    row = lax.broadcasted_iota(jnp.int32, (padded, campaigns), 0)
    wanted = lax.broadcasted_iota(jnp.int32, (padded, campaigns), 1) - lax.rem(row, w)
    wanted = jnp.where(row < blocks * rows, wanted, -2 * TILE).astype(jnp.float32)
    ones = jnp.ones((TILE, campaigns), jnp.bfloat16)

    @pl.loop(0, devices // UNROLL)
    def _(step):
        for n in range(UNROLL):
            i = step * UNROLL + n
            ids = packets_ref[i, lines : lines + LINES, :].astype(jnp.float32)
            spread = jnp.zeros((padded, TILE), jnp.float32)
            for b in range(blocks):
                mine = jnp.logical_and(own_slot, row_block == b)
                spread = jnp.where(mine, ids[b : b + 1, :], spread)
                acts_ref[i, b * ACT : b * ACT + hours, :] = packets_ref[i, act_row + b * hours : act_row + (b + 1) * hours, :]
                acts_ref[i, b * ACT + hours : (b + 1) * ACT, :] = tail
            first = jnp.dot(spread.astype(jnp.bfloat16), ones, preferred_element_type=jnp.float32)
            hot_ref[i] = jnp.where(first == wanted, 1.0, 0.0).astype(jnp.bfloat16)


def usage_at(lam, blocks, rows, packets_ref, hot_ref, acts_ref, named_ref, share_ref, used_ref):
    hours, campaigns = lam.shape
    devices, padded = hot_ref.shape[:2]
    chunk = share_ref.shape[0]
    listed = blocks * rows
    hour = lax.broadcasted_iota(jnp.int32, (ACT - hours, campaigns), 0)
    half = jnp.where(hour == 0, 0.5, 0.0)
    table = jnp.concatenate([rounded(lam) * -0.5, half] * blocks, axis=0).astype(jnp.bfloat16)
    row = lax.broadcasted_iota(jnp.int32, (listed, blocks * ACT), 0)
    own = row // rows == lax.broadcasted_iota(jnp.int32, (listed, blocks * ACT), 1) // ACT
    block = lax.broadcasted_iota(jnp.int32, (ACT, padded), 1) // rows
    if listed < padded:
        share_ref[:, listed:, :] = jnp.zeros((chunk, padded - listed, TILE), jnp.bfloat16)

    def senders(step, total):
        first = step * chunk
        hot = [hot_ref[first + n, :listed, :] for n in range(chunk)]
        for n in range(chunk):
            named = lax.dot_general(hot[n], table, NT, preferred_element_type=jnp.float32)
            named_ref[n] = jnp.where(own, named, 0.0).astype(jnp.bfloat16)
        for n in range(chunk):
            part = jnp.dot(named_ref[n], acts_ref[first + n], preferred_element_type=jnp.float32)
            score = packets_ref[first + n, :listed, :].astype(jnp.float32)
            share_ref[n, :listed, :] = jnp.clip(score + part, 0.0, 1.0).astype(jnp.bfloat16)
        for n in range(chunk):
            each = lax.dot_general(acts_ref[first + n], share_ref[n], NT, preferred_element_type=jnp.float32)
            used = each[:ACT]
            for b in range(1, blocks):
                used = jnp.where(block == b, each[b * ACT : (b + 1) * ACT], used)
            high = rounded(used)
            both = jnp.concatenate([high, used - high], axis=0).astype(jnp.bfloat16)
            used_ref[:, n * padded : (n + 1) * padded] = both
        hot = hot_ref[pl.ds(first, chunk)].reshape(chunk * padded, campaigns)
        return total + jnp.dot(used_ref[...], hot, preferred_element_type=jnp.float32)

    total = jnp.zeros((2 * ACT, campaigns), jnp.float32)
    total = lax.fori_loop(0, devices // chunk, senders, total)
    return total[:hours] + total[ACT : ACT + hours]


def scale_of(parts_ref, entries):
    squares = jnp.sum(jnp.sum(parts_ref[:, 0, :], axis=0, keepdims=True), axis=1, keepdims=True)
    return lax.rsqrt(squares / entries + 1e-06)


def moved(lam, gap, scale):
    return jnp.maximum(lam + 0.3 * (gap * scale), 0.0)


def direction_kernel(blocks, rows, entries, kind, *refs):
    refs, scratch = refs[:-3], refs[-3:]
    if kind == "first":
        packets_ref, gap_ref, send_ref, anchor_ref, limit_ref, hot_ref, acts_ref = refs
        hours = gap_ref.shape[0]
        unpack(hours, blocks, rows, packets_ref, anchor_ref, limit_ref, hot_ref, acts_ref)
        at = anchor_ref[...]
    elif kind == "middle":
        packets_ref, anchor_ref, limit_ref, hot_ref, acts_ref, before_ref, sums_ref, gap_ref, send_ref = refs
        at = moved(anchor_ref[...], before_ref[...], scale_of(sums_ref, entries))
    elif kind == "last":
        packets_ref, anchor_ref, limit_ref, hot_ref, acts_ref, lam_ref, before_ref, sums_ref, send_ref = refs
        at = moved(lam_ref[...], before_ref[...], scale_of(sums_ref, entries))
    else:
        packets_ref, anchor_ref, limit_ref, hot_ref, acts_ref = refs[:5]
        lam_ref, before_ref, sums_ref, gap_ref, send_ref, lam_out_ref = refs[5:]
        extra = moved(lam_ref[...], before_ref[...], scale_of(sums_ref, entries))
        weight = 1.0 / (kind + 2.0)
        at = weight * anchor_ref[...] + (1.0 - weight) * extra
        lam_out_ref[...] = at
    gap = usage_at(at, blocks, rows, packets_ref, hot_ref, acts_ref, *scratch) - limit_ref[...]
    line = jnp.sum(gap * gap, axis=0, keepdims=True)
    if kind != "last":
        gap_ref[...] = gap
        line = sum(line[:, n : n + TILE] for n in range(0, line.shape[1], TILE))
        send_ref[...] = jnp.broadcast_to(line[None], send_ref.shape)
        return
    hours, campaigns = gap.shape
    devices, span = send_ref.shape[:2]
    squares = jnp.broadcast_to(jnp.sum(line, axis=1, keepdims=True), (LINES, campaigns))
    results = [gap, lam_ref[...]]
    results.append(jnp.zeros((SUM_LANE - 2 * hours, campaigns), jnp.float32))
    results.append(squares)
    results.append(jnp.zeros((TILE - SUM_LANE - LINES, campaigns), jnp.float32))
    results = jnp.concatenate(results, axis=0).T
    for i in range(devices):
        send_ref[i] = results[i * span : (i + 1) * span]


def fold_kernel(last, parts_ref, out_ref):
    line = jnp.sum(parts_ref[:, 0, :], axis=0, keepdims=True)
    if last:
        lane = lax.broadcasted_iota(jnp.int32, line.shape, 1)
        line = jnp.where(lane == SUM_LANE, line, 0.0)
    out_ref[...] = jnp.broadcast_to(line[None], out_ref.shape)


def final_kernel(entries, step, anchor_ref, parts_ref, sums_ref, new_ref, dir_ref, rows):
    devices, span = parts_ref.shape[:2]
    hours, campaigns = anchor_ref.shape
    w = TILE // devices
    for m in range(devices):
        for j in range(span // w):
            rows[j * TILE + m * w : j * TILE + (m + 1) * w, :] = parts_ref[m, j * w : (j + 1) * w, :]
    results = rows[...].T
    gap, lam = results[:hours], results[hours : 2 * hours]
    scale = scale_of(sums_ref, entries)
    dir_ref[...] = gap * scale
    weight = 1.0 / (step + 2.0)
    new_ref[...] = weight * anchor_ref[...] + (1.0 - weight) * moved(lam, gap, scale)


def swapped(parts, axis):
    return lax.all_to_all(parts, axis, split_axis=0, concat_axis=0, tiled=True)


def kernel_call(body, name, out_shape, in_specs, out_specs, scratch_shapes=()):
    return pl.pallas_call(
        body,
        out_shape=out_shape,
        in_specs=in_specs,
        out_specs=out_specs,
        scratch_shapes=scratch_shapes,
        compiler_params=PARAMS,
        name=name,
    )


def on_device(scores, elig_ids, elig_counts, activity, prices, spend_limit):
    devices = lax.axis_size(USERS)
    groups = lax.axis_size("camps")
    entries = float(prices.size * devices * groups)
    hours, campaigns = prices.shape
    blocks, slots = scores.shape[0], scores.shape[2]
    w = TILE // devices
    span = campaigns // TILE * w
    rows = slots * w
    padded = pl.cdiv(blocks * rows, TILE) * TILE
    chunk = min(CHUNK, devices)
    bf16, f32, i32 = jnp.bfloat16, jnp.float32, jnp.int32
    shape = jax.ShapeDtypeStruct

    sources = (scores, elig_ids, elig_counts[:, 0], prices, spend_limit, activity)
    packets = kernel_call(
        cut_kernel,
        "cut",
        shape((devices, blocks * (rows + hours) + span + LINES, TILE), bf16),
        [HBM] * len(sources),
        VMEM,
        [
            pltpu.VMEM(scores.shape, bf16),
            pltpu.SMEM(elig_ids.shape, i32),
            pltpu.SMEM((blocks,), i32),
            pltpu.VMEM(prices.shape, f32),
            pltpu.VMEM(prices.shape, f32),
            pltpu.VMEM(activity.shape, bf16),
            pltpu.SemaphoreType.DMA((len(sources),)),
        ],
    )(*(pltpu.with_memory_space_constraint(source, pltpu.HBM) for source in sources))
    packets = swapped(packets, USERS)

    value = shape(prices.shape, f32)
    part = shape((devices, 1, TILE), f32)

    def total_of(parts, last=False):
        folded = kernel_call(
            functools.partial(fold_kernel, last), "fold", shape((groups, 1, TILE), f32), [VMEM], VMEM
        )(parts)
        return swapped(folded, "camps")

    def direction(kind, outs, *args):
        return kernel_call(
            functools.partial(direction_kernel, blocks, rows, entries, kind),
            "direction",
            outs,
            [VMEM] * len(args),
            [VMEM] * len(outs),
            [
                pltpu.VMEM((chunk, blocks * rows, blocks * ACT), bf16),
                pltpu.VMEM((chunk, padded, TILE), bf16),
                pltpu.VMEM((2 * ACT, chunk * padded), bf16),
            ],
        )(*args)

    kept_shapes = [
        value,
        value,
        shape((devices, padded, campaigns), bf16),
        shape((devices, blocks * ACT, TILE), bf16),
    ]
    gap, parts, *kept = direction("first", [value, part] + kept_shapes, packets)
    lam = kept[0]
    for step in range(STEPS - 1):
        sums = total_of(swapped(parts, USERS))
        gap, parts = direction("middle", [value, part], packets, *kept, gap, sums)
        sums = total_of(swapped(parts, USERS))
        gap, parts, lam = direction(step, [value, part, value], packets, *kept, lam, gap, sums)
    sums = total_of(swapped(parts, USERS))
    (parts,) = direction("last", [shape((devices, span, TILE), f32)], packets, *kept, lam, gap, sums)
    parts = swapped(parts, USERS)
    new, last = kernel_call(
        functools.partial(final_kernel, entries, STEPS - 1),
        "final",
        [value, value],
        [VMEM] * 3,
        [VMEM] * 2,
        [pltpu.VMEM((campaigns, TILE), f32)],
    )(prices, parts, total_of(parts, last=True))
    return (new, last)


def solution(mesh):
    torus = Mesh(
        mesh.devices.reshape(4, 4, 2, mesh.shape["camps"]),
        ("users_0", "users_1", "users_2", "camps"),
    )
    in_specs = (
        P(USERS, "camps", None, None, None),
        P(USERS, "camps", None),
        P(USERS, "camps"),
        P(None, USERS),
        P(None, USERS_CAMPS),
        P(None, USERS_CAMPS),
    )
    out_specs = (P(None, USERS_CAMPS), P(None, USERS_CAMPS))
    return jax.shard_map(
        on_device, mesh=torus, in_specs=in_specs, out_specs=out_specs, check_vma=False
    )
```

```python
import functools

import jax
import jax.numpy as jnp
from jax import lax
from jax.experimental import pallas as pl
from jax.experimental.pallas import tpu as pltpu
from jax.sharding import Mesh
from jax.sharding import PartitionSpec as P

STEPS = 2
USERS = ("users_0", "users_1", "users_2")
USERS_CAMPS = ("users_0", "users_1", "users_2", "camps")
TILE = 128
LINES = 8
TERMS = 5
ACT = 32
CHUNK = 32
UNROLL = 8
SUM_LANE = 64

VMEM = pl.BlockSpec(memory_space=pltpu.VMEM)
HBM = pl.BlockSpec(memory_space=pltpu.HBM)
PARAMS = pltpu.CompilerParams(vmem_limit_bytes=8 * 2**20)
NT = (((1,), (1,)), ((), ()))


def entry_place(hours, slots, block, slot):
    free = TILE - TERMS * hours
    return block * ((slots + free - 1) // free) + slot // free, TERMS * hours + slot % free


def rounded(value):
    return value.astype(jnp.bfloat16).astype(jnp.float32)


def cut_kernel(scores_hbm, ids_hbm, counts_hbm, prices_hbm, limit_hbm, act_hbm, out_ref, *scratch):
    scores, ids, counts, prices, limits, act, sems = scratch
    sources = (scores_hbm, ids_hbm, counts_hbm, prices_hbm, limit_hbm, act_hbm)
    loads = [pltpu.make_async_copy(sources[n], scratch[n], sems.at[n]) for n in range(len(sources))]
    for load in loads:
        load.start()
    devices = out_ref.shape[0]
    hours, campaigns = prices.shape
    blocks, slots = scores.shape[0], scores.shape[2]
    owned = campaigns // TILE
    w = TILE // devices
    span = owned * w
    acts = blocks * slots * w
    values = acts + blocks * hours
    row = lax.broadcasted_iota(jnp.int32, (campaigns, campaigns), 0)
    col = lax.broadcasted_iota(jnp.int32, (campaigns, campaigns), 1)
    source = lax.rem(row, span) // w * TILE + row // span * w + lax.rem(row, w)
    pick = jnp.where(col == source, 1.0, 0.0)
    pick_half = (pick * 0.5).astype(jnp.bfloat16)
    pick = pick.astype(jnp.bfloat16)

    loads[3].wait()
    loads[4].wait()
    price, limit = prices[...], limits[...]
    high = rounded(price)
    middle = rounded(price - high)
    limit_high = rounded(limit)
    terms = [high, middle, price - high - middle, limit_high, limit - limit_high]
    terms.append(jnp.zeros((TILE - len(terms) * hours, campaigns), jnp.float32))
    terms = jnp.concatenate(terms, axis=0).astype(jnp.bfloat16)
    terms = lax.dot_general(pick, terms, NT, preferred_element_type=jnp.float32)
    loads[1].wait()
    loads[2].wait()
    row = lax.broadcasted_iota(jnp.int32, (span, TILE), 0)
    lane = lax.broadcasted_iota(jnp.int32, (span, TILE), 1)
    entries = jnp.full((span, TILE), -TILE, jnp.int32)
    for b in range(blocks):
        for k in range(slots):
            at_row, at_lane = entry_place(hours, slots, b, k)
            here = jnp.logical_and(row == at_row, lane == at_lane)
            entries = jnp.where(here, jnp.where(k < counts[b], ids[b, 0, k] * w, -TILE), entries)
    entries = jnp.concatenate([entries.astype(jnp.float32)] * devices, axis=0)
    lane = lax.broadcasted_iota(jnp.int32, terms.shape, 1)
    terms = jnp.where(lane < TERMS * hours, terms, entries).astype(jnp.bfloat16)
    for m in range(devices):
        out_ref[m, values : values + span, :] = terms[m * span : (m + 1) * span]
    loads[5].wait()
    for b in range(blocks):
        own = act[:, b * TILE : (b + 1) * TILE]
        for m in range(devices):
            out_ref[m, acts + b * hours : acts + (b + 1) * hours, :] = own
    loads[0].wait()
    for b in range(blocks):
        for k in range(0, slots, owned):
            tiles = jnp.concatenate([scores[b, 0, k + j] for j in range(owned)], axis=1)
            cut = lax.dot_general(pick_half, tiles, NT, preferred_element_type=jnp.float32).astype(jnp.bfloat16)
            at = (b * slots + k) * w
            for m in range(devices):
                out_ref[m, at : at + span, :] = cut[m * span : (m + 1) * span]


def unpack(hours, blocks, rows, packets_ref, anchor_ref, limit_ref, hot_ref, acts_ref):
    devices = packets_ref.shape[0]
    campaigns = anchor_ref.shape[1]
    span = campaigns // devices
    w = TILE // devices
    act_row = blocks * rows
    values = act_row + blocks * hours
    slots = rows // w
    terms = packets_ref[:, values : values + span, :].reshape(campaigns, TILE).astype(jnp.float32).T
    terms = [terms[n * hours : (n + 1) * hours] for n in range(TERMS)]
    anchor_ref[...] = terms[0] + terms[1] + terms[2]
    limit_ref[...] = terms[3] + terms[4]
    hour = lax.broadcasted_iota(jnp.int32, (ACT - hours, TILE), 0)
    tail = jnp.where(hour == 0, 1.0, 0.0).astype(jnp.bfloat16)
    padded = hot_ref.shape[1]
    row = lax.broadcasted_iota(jnp.int32, (padded, TILE), 0)
    lane = lax.broadcasted_iota(jnp.int32, (padded, TILE), 1)
    at_row, at_lane = entry_place(hours, slots, row // rows, lax.rem(row, rows) // w)
    at_row = jnp.where(lane == at_lane, at_row, -1)
    lines = entry_place(hours, slots, blocks - 1, slots - 1)[0] + 1
    row = lax.broadcasted_iota(jnp.int32, (padded, campaigns), 0)
    wanted = lax.broadcasted_iota(jnp.int32, (padded, campaigns), 1) - lax.rem(row, w)
    wanted = jnp.where(row < blocks * rows, wanted, -2 * TILE).astype(jnp.float32)
    ones = jnp.ones((TILE, campaigns), jnp.bfloat16)

    @pl.loop(0, devices // UNROLL)
    def _(step):
        for n in range(UNROLL):
            i = step * UNROLL + n
            ids = packets_ref[i, values : values + span, :].astype(jnp.float32)
            spread = jnp.zeros((padded, TILE), jnp.float32)
            for r in range(lines):
                spread = jnp.where(at_row == r, ids[r : r + 1, :], spread)
            for b in range(blocks):
                acts_ref[i, b * ACT : b * ACT + hours, :] = packets_ref[i, act_row + b * hours : act_row + (b + 1) * hours, :]
                acts_ref[i, b * ACT + hours : (b + 1) * ACT, :] = tail
            first = jnp.dot(spread.astype(jnp.bfloat16), ones, preferred_element_type=jnp.float32)
            hot_ref[i] = jnp.where(first == wanted, 1.0, 0.0).astype(jnp.bfloat16)


def usage_at(lam, blocks, rows, packets_ref, hot_ref, acts_ref, named_ref, share_ref, used_ref):
    hours, campaigns = lam.shape
    devices, padded = hot_ref.shape[:2]
    chunk = share_ref.shape[0]
    listed = blocks * rows
    hour = lax.broadcasted_iota(jnp.int32, (ACT - hours, campaigns), 0)
    half = jnp.where(hour == 0, 0.5, 0.0)
    table = jnp.concatenate([rounded(lam) * -0.5, half] * blocks, axis=0).astype(jnp.bfloat16)
    row = lax.broadcasted_iota(jnp.int32, (listed, blocks * ACT), 0)
    own = row // rows == lax.broadcasted_iota(jnp.int32, (listed, blocks * ACT), 1) // ACT
    block = lax.broadcasted_iota(jnp.int32, (ACT, padded), 1) // rows
    if listed < padded:
        share_ref[:, :, listed:] = jnp.zeros((chunk, TILE, padded - listed), jnp.bfloat16)

    def senders(step, total):
        first = step * chunk
        hot = [hot_ref[first + n, :listed, :] for n in range(chunk)]
        for n in range(chunk):
            named = lax.dot_general(hot[n], table, NT, preferred_element_type=jnp.float32)
            named_ref[n] = jnp.where(own, named, 0.0).astype(jnp.bfloat16)
        for n in range(chunk):
            part = jnp.dot(named_ref[n], acts_ref[first + n], preferred_element_type=jnp.float32)
            score = packets_ref[first + n, :listed, :].astype(jnp.float32)
            share_ref[n, :, :listed] = jnp.clip(score + part, 0.0, 1.0).astype(jnp.bfloat16).T
        for n in range(chunk):
            each = jnp.dot(acts_ref[first + n], share_ref[n], preferred_element_type=jnp.float32)
            used = each[:ACT]
            for b in range(1, blocks):
                used = jnp.where(block == b, each[b * ACT : (b + 1) * ACT], used)
            high = rounded(used)
            both = jnp.concatenate([high, used - high], axis=0).astype(jnp.bfloat16)
            used_ref[:, n * padded : (n + 1) * padded] = both
        hot = hot_ref[pl.ds(first, chunk)].reshape(chunk * padded, campaigns)
        return total + jnp.dot(used_ref[...], hot, preferred_element_type=jnp.float32)

    total = jnp.zeros((2 * ACT, campaigns), jnp.float32)
    total = lax.fori_loop(0, devices // chunk, senders, total)
    return total[:hours] + total[ACT : ACT + hours]


def scale_of(parts_ref, entries):
    squares = jnp.sum(jnp.sum(parts_ref[:, 0, :], axis=0, keepdims=True), axis=1, keepdims=True)
    return lax.rsqrt(squares / entries + 1e-06)


def moved(lam, gap, scale):
    return jnp.maximum(lam + 0.3 * (gap * scale), 0.0)


def direction_kernel(blocks, rows, entries, kind, *refs):
    refs, scratch = refs[:-3], refs[-3:]
    if kind == "first":
        packets_ref, gap_ref, send_ref, anchor_ref, limit_ref, hot_ref, acts_ref = refs
        hours = gap_ref.shape[0]
        unpack(hours, blocks, rows, packets_ref, anchor_ref, limit_ref, hot_ref, acts_ref)
        at = anchor_ref[...]
    elif kind == "middle":
        packets_ref, anchor_ref, limit_ref, hot_ref, acts_ref, before_ref, sums_ref, gap_ref, send_ref = refs
        at = moved(anchor_ref[...], before_ref[...], scale_of(sums_ref, entries))
    elif kind == "last":
        packets_ref, anchor_ref, limit_ref, hot_ref, acts_ref, lam_ref, before_ref, sums_ref, send_ref = refs
        at = moved(lam_ref[...], before_ref[...], scale_of(sums_ref, entries))
    else:
        packets_ref, anchor_ref, limit_ref, hot_ref, acts_ref = refs[:5]
        lam_ref, before_ref, sums_ref, gap_ref, send_ref, lam_out_ref = refs[5:]
        extra = moved(lam_ref[...], before_ref[...], scale_of(sums_ref, entries))
        weight = 1.0 / (kind + 2.0)
        at = weight * anchor_ref[...] + (1.0 - weight) * extra
        lam_out_ref[...] = at
    gap = usage_at(at, blocks, rows, packets_ref, hot_ref, acts_ref, *scratch) - limit_ref[...]
    line = jnp.sum(gap * gap, axis=0, keepdims=True)
    if kind != "last":
        gap_ref[...] = gap
        line = sum(line[:, n : n + TILE] for n in range(0, line.shape[1], TILE))
        send_ref[...] = jnp.broadcast_to(line[None], send_ref.shape)
        return
    hours, campaigns = gap.shape
    devices, span = send_ref.shape[:2]
    squares = jnp.broadcast_to(jnp.sum(line, axis=1, keepdims=True), (LINES, campaigns))
    results = [gap, lam_ref[...]]
    results.append(jnp.zeros((SUM_LANE - 2 * hours, campaigns), jnp.float32))
    results.append(squares)
    results.append(jnp.zeros((TILE - SUM_LANE - LINES, campaigns), jnp.float32))
    results = jnp.concatenate(results, axis=0).T
    for i in range(devices):
        send_ref[i] = results[i * span : (i + 1) * span]


def fold_kernel(last, parts_ref, out_ref):
    line = jnp.sum(parts_ref[:, 0, :], axis=0, keepdims=True)
    if last:
        lane = lax.broadcasted_iota(jnp.int32, line.shape, 1)
        line = jnp.where(lane == SUM_LANE, line, 0.0)
    out_ref[...] = jnp.broadcast_to(line[None], out_ref.shape)


def final_kernel(entries, step, anchor_ref, parts_ref, sums_ref, new_ref, dir_ref, rows):
    devices, span = parts_ref.shape[:2]
    hours, campaigns = anchor_ref.shape
    w = TILE // devices
    for m in range(devices):
        for j in range(span // w):
            rows[j * TILE + m * w : j * TILE + (m + 1) * w, :] = parts_ref[m, j * w : (j + 1) * w, :]
    results = rows[...].T
    gap, lam = results[:hours], results[hours : 2 * hours]
    scale = scale_of(sums_ref, entries)
    dir_ref[...] = gap * scale
    weight = 1.0 / (step + 2.0)
    new_ref[...] = weight * anchor_ref[...] + (1.0 - weight) * moved(lam, gap, scale)


def swapped(parts, axis):
    return lax.all_to_all(parts, axis, split_axis=0, concat_axis=0, tiled=True)


def kernel_call(body, name, out_shape, in_specs, out_specs, scratch_shapes=()):
    return pl.pallas_call(
        body,
        out_shape=out_shape,
        in_specs=in_specs,
        out_specs=out_specs,
        scratch_shapes=scratch_shapes,
        compiler_params=PARAMS,
        name=name,
    )


def on_device(scores, elig_ids, elig_counts, activity, prices, spend_limit):
    devices = lax.axis_size(USERS)
    groups = lax.axis_size("camps")
    entries = float(prices.size * devices * groups)
    hours, campaigns = prices.shape
    blocks, slots = scores.shape[0], scores.shape[2]
    w = TILE // devices
    span = campaigns // TILE * w
    rows = slots * w
    padded = pl.cdiv(blocks * rows, TILE) * TILE
    chunk = min(CHUNK, devices)
    bf16, f32, i32 = jnp.bfloat16, jnp.float32, jnp.int32
    shape = jax.ShapeDtypeStruct

    sources = (scores, elig_ids, elig_counts[:, 0], prices, spend_limit, activity)
    packets = kernel_call(
        cut_kernel,
        "cut",
        shape((devices, blocks * (rows + hours) + span, TILE), bf16),
        [HBM] * len(sources),
        VMEM,
        [
            pltpu.VMEM(scores.shape, bf16),
            pltpu.SMEM(elig_ids.shape, i32),
            pltpu.SMEM((blocks,), i32),
            pltpu.VMEM(prices.shape, f32),
            pltpu.VMEM(prices.shape, f32),
            pltpu.VMEM(activity.shape, bf16),
            pltpu.SemaphoreType.DMA((len(sources),)),
        ],
    )(*(pltpu.with_memory_space_constraint(source, pltpu.HBM) for source in sources))
    packets = swapped(packets, USERS)

    value = shape(prices.shape, f32)
    part = shape((devices, 1, TILE), f32)

    def total_of(parts, last=False):
        folded = kernel_call(
            functools.partial(fold_kernel, last), "fold", shape((groups, 1, TILE), f32), [VMEM], VMEM
        )(parts)
        return swapped(folded, "camps")

    def direction(kind, outs, *args):
        return kernel_call(
            functools.partial(direction_kernel, blocks, rows, entries, kind),
            "direction",
            outs,
            [VMEM] * len(args),
            [VMEM] * len(outs),
            [
                pltpu.VMEM((chunk, blocks * rows, blocks * ACT), bf16),
                pltpu.VMEM((chunk, TILE, padded), bf16),
                pltpu.VMEM((2 * ACT, chunk * padded), bf16),
            ],
        )(*args)

    kept_shapes = [
        value,
        value,
        shape((devices, padded, campaigns), bf16),
        shape((devices, blocks * ACT, TILE), bf16),
    ]
    gap, parts, *kept = direction("first", [value, part] + kept_shapes, packets)
    lam = kept[0]
    for step in range(STEPS - 1):
        sums = total_of(swapped(parts, USERS))
        gap, parts = direction("middle", [value, part], packets, *kept, gap, sums)
        sums = total_of(swapped(parts, USERS))
        gap, parts, lam = direction(step, [value, part, value], packets, *kept, lam, gap, sums)
    sums = total_of(swapped(parts, USERS))
    (parts,) = direction("last", [shape((devices, span, TILE), f32)], packets, *kept, lam, gap, sums)
    parts = swapped(parts, USERS)
    new, last = kernel_call(
        functools.partial(final_kernel, entries, STEPS - 1),
        "final",
        [value, value],
        [VMEM] * 3,
        [VMEM] * 2,
        [pltpu.VMEM((campaigns, TILE), f32)],
    )(prices, parts, total_of(parts, last=True))
    return (new, last)


def solution(mesh):
    torus = Mesh(
        mesh.devices.reshape(4, 4, 2, mesh.shape["camps"]),
        ("users_0", "users_1", "users_2", "camps"),
    )
    in_specs = (
        P(USERS, "camps", None, None, None),
        P(USERS, "camps", None),
        P(USERS, "camps"),
        P(None, USERS),
        P(None, USERS_CAMPS),
        P(None, USERS_CAMPS),
    )
    out_specs = (P(None, USERS_CAMPS), P(None, USERS_CAMPS))
    return jax.shard_map(
        on_device, mesh=torus, in_specs=in_specs, out_specs=out_specs, check_vma=False
    )
```

```python
import functools

import jax
import jax.numpy as jnp
from jax import lax
from jax.experimental import pallas as pl
from jax.experimental.pallas import tpu as pltpu
from jax.sharding import Mesh
from jax.sharding import PartitionSpec as P

STEPS = 2
USERS = ("users_0", "users_1", "users_2")
USERS_CAMPS = ("users_0", "users_1", "users_2", "camps")
TILE = 128
LINES = 8
TERMS = 5
ACT = 32
CHUNK = 32
UNROLL = 32
SUM_LANE = 64

VMEM = pl.BlockSpec(memory_space=pltpu.VMEM)
HBM = pl.BlockSpec(memory_space=pltpu.HBM)
PARAMS = pltpu.CompilerParams(vmem_limit_bytes=8 * 2**20)
NT = (((1,), (1,)), ((), ()))


def entry_place(hours, slots, block, slot):
    free = TILE - TERMS * hours
    return block * ((slots + free - 1) // free) + slot // free, TERMS * hours + slot % free


def rounded(value):
    return value.astype(jnp.bfloat16).astype(jnp.float32)


def cut_kernel(scores_hbm, ids_hbm, counts_hbm, prices_hbm, limit_hbm, act_hbm, out_ref, *scratch):
    scores, ids, counts, prices, limits, act, sems = scratch
    sources = (scores_hbm, ids_hbm, counts_hbm, prices_hbm, limit_hbm, act_hbm)
    loads = [pltpu.make_async_copy(sources[n], scratch[n], sems.at[n]) for n in range(len(sources))]
    for load in loads:
        load.start()
    devices = out_ref.shape[0]
    hours, campaigns = prices.shape
    blocks, slots = scores.shape[0], scores.shape[2]
    owned = campaigns // TILE
    w = TILE // devices
    span = owned * w
    acts = blocks * slots * w
    values = acts + blocks * hours
    row = lax.broadcasted_iota(jnp.int32, (campaigns, campaigns), 0)
    col = lax.broadcasted_iota(jnp.int32, (campaigns, campaigns), 1)
    source = lax.rem(row, span) // w * TILE + row // span * w + lax.rem(row, w)
    pick = jnp.where(col == source, 1.0, 0.0)
    pick_half = (pick * 0.5).astype(jnp.bfloat16)
    pick = pick.astype(jnp.bfloat16)

    loads[3].wait()
    loads[4].wait()
    price, limit = prices[...], limits[...]
    high = rounded(price)
    middle = rounded(price - high)
    limit_high = rounded(limit)
    terms = [high, middle, price - high - middle, limit_high, limit - limit_high]
    terms.append(jnp.zeros((TILE - len(terms) * hours, campaigns), jnp.float32))
    terms = jnp.concatenate(terms, axis=0).astype(jnp.bfloat16)
    terms = lax.dot_general(pick, terms, NT, preferred_element_type=jnp.float32)
    loads[1].wait()
    loads[2].wait()
    row = lax.broadcasted_iota(jnp.int32, (span, TILE), 0)
    lane = lax.broadcasted_iota(jnp.int32, (span, TILE), 1)
    entries = jnp.full((span, TILE), -TILE, jnp.int32)
    for b in range(blocks):
        for k in range(slots):
            at_row, at_lane = entry_place(hours, slots, b, k)
            here = jnp.logical_and(row == at_row, lane == at_lane)
            entries = jnp.where(here, jnp.where(k < counts[b], ids[b, 0, k] * w, -TILE), entries)
    entries = jnp.concatenate([entries.astype(jnp.float32)] * devices, axis=0)
    lane = lax.broadcasted_iota(jnp.int32, terms.shape, 1)
    terms = jnp.where(lane < TERMS * hours, terms, entries).astype(jnp.bfloat16)
    for m in range(devices):
        out_ref[m, values : values + span, :] = terms[m * span : (m + 1) * span]
    loads[5].wait()
    for b in range(blocks):
        own = act[:, b * TILE : (b + 1) * TILE]
        for m in range(devices):
            out_ref[m, acts + b * hours : acts + (b + 1) * hours, :] = own
    loads[0].wait()
    for b in range(blocks):
        for k in range(0, slots, owned):
            tiles = jnp.concatenate([scores[b, 0, k + j] for j in range(owned)], axis=1)
            cut = lax.dot_general(pick_half, tiles, NT, preferred_element_type=jnp.float32).astype(jnp.bfloat16)
            at = (b * slots + k) * w
            for m in range(devices):
                out_ref[m, at : at + span, :] = cut[m * span : (m + 1) * span]


def unpack(hours, blocks, rows, packets_ref, anchor_ref, limit_ref, hot_ref, acts_ref):
    devices = packets_ref.shape[0]
    campaigns = anchor_ref.shape[1]
    span = campaigns // devices
    w = TILE // devices
    act_row = blocks * rows
    values = act_row + blocks * hours
    slots = rows // w
    terms = packets_ref[:, values : values + span, :].reshape(campaigns, TILE).astype(jnp.float32).T
    terms = [terms[n * hours : (n + 1) * hours] for n in range(TERMS)]
    anchor_ref[...] = terms[0] + terms[1] + terms[2]
    limit_ref[...] = terms[3] + terms[4]
    hour = lax.broadcasted_iota(jnp.int32, (ACT - hours, TILE), 0)
    tail = jnp.where(hour == 0, 1.0, 0.0).astype(jnp.bfloat16)
    padded = hot_ref.shape[1]
    row = lax.broadcasted_iota(jnp.int32, (padded, TILE), 0)
    lane = lax.broadcasted_iota(jnp.int32, (padded, TILE), 1)
    at_row, at_lane = entry_place(hours, slots, row // rows, lax.rem(row, rows) // w)
    at_row = jnp.where(lane == at_lane, at_row, -1)
    lines = entry_place(hours, slots, blocks - 1, slots - 1)[0] + 1
    row = lax.broadcasted_iota(jnp.int32, (padded, campaigns), 0)
    wanted = lax.broadcasted_iota(jnp.int32, (padded, campaigns), 1) - lax.rem(row, w)
    wanted = jnp.where(row < blocks * rows, wanted, -2 * TILE).astype(jnp.float32)
    ones = jnp.ones((TILE, TILE), jnp.bfloat16)

    @pl.loop(0, devices // UNROLL)
    def _(step):
        for n in range(UNROLL):
            i = step * UNROLL + n
            ids = packets_ref[i, values : values + span, :].astype(jnp.float32)
            spread = jnp.zeros((padded, TILE), jnp.float32)
            for r in range(lines):
                spread = jnp.where(at_row == r, ids[r : r + 1, :], spread)
            for b in range(blocks):
                acts_ref[i, b * ACT : b * ACT + hours, :] = packets_ref[i, act_row + b * hours : act_row + (b + 1) * hours, :]
                acts_ref[i, b * ACT + hours : (b + 1) * ACT, :] = tail
            first = jnp.dot(spread.astype(jnp.bfloat16), ones, preferred_element_type=jnp.float32)
            first = jnp.concatenate([first] * (campaigns // TILE), axis=1)
            hot_ref[i] = jnp.where(first == wanted, 1.0, 0.0).astype(jnp.bfloat16)


def usage_at(lam, blocks, rows, packets_ref, hot_ref, acts_ref, named_ref, share_ref, used_ref):
    hours, campaigns = lam.shape
    devices, padded = hot_ref.shape[:2]
    chunk = share_ref.shape[0]
    listed = blocks * rows
    hour = lax.broadcasted_iota(jnp.int32, (ACT - hours, campaigns), 0)
    half = jnp.where(hour == 0, 0.5, 0.0)
    table = jnp.concatenate([rounded(lam) * -0.5, half] * blocks, axis=0).astype(jnp.bfloat16)
    row = lax.broadcasted_iota(jnp.int32, (listed, blocks * ACT), 0)
    own = row // rows == lax.broadcasted_iota(jnp.int32, (listed, blocks * ACT), 1) // ACT
    block = lax.broadcasted_iota(jnp.int32, (ACT, padded), 1) // rows
    if listed < padded:
        share_ref[:, :, listed:] = jnp.zeros((chunk, TILE, padded - listed), jnp.bfloat16)

    def senders(step, total):
        first = step * chunk
        hot = [hot_ref[first + n, :listed, :] for n in range(chunk)]
        for n in range(chunk):
            named = lax.dot_general(hot[n], table, NT, preferred_element_type=jnp.float32)
            named_ref[n] = jnp.where(own, named, 0.0).astype(jnp.bfloat16)
        for n in range(chunk):
            part = jnp.dot(named_ref[n], acts_ref[first + n], preferred_element_type=jnp.float32)
            score = packets_ref[first + n, :listed, :].astype(jnp.float32)
            share_ref[n, :, :listed] = jnp.clip(score + part, 0.0, 1.0).astype(jnp.bfloat16).T
        for n in range(chunk):
            each = jnp.dot(acts_ref[first + n], share_ref[n], preferred_element_type=jnp.float32)
            used = each[:ACT]
            for b in range(1, blocks):
                used = jnp.where(block == b, each[b * ACT : (b + 1) * ACT], used)
            high = rounded(used)
            both = jnp.concatenate([high, used - high], axis=0).astype(jnp.bfloat16)
            used_ref[:, n * padded : (n + 1) * padded] = both
        hot = hot_ref[pl.ds(first, chunk)].reshape(chunk * padded, campaigns)
        return total + jnp.dot(used_ref[...], hot, preferred_element_type=jnp.float32)

    total = jnp.zeros((2 * ACT, campaigns), jnp.float32)
    total = lax.fori_loop(0, devices // chunk, senders, total)
    return total[:hours] + total[ACT : ACT + hours]


def scale_of(parts_ref, entries):
    squares = jnp.sum(jnp.sum(parts_ref[:, 0, :], axis=0, keepdims=True), axis=1, keepdims=True)
    return lax.rsqrt(squares / entries + 1e-06)


def moved(lam, gap, scale):
    return jnp.maximum(lam + 0.3 * (gap * scale), 0.0)


def direction_kernel(blocks, rows, entries, kind, *refs):
    refs, scratch = refs[:-3], refs[-3:]
    if kind == "first":
        packets_ref, gap_ref, send_ref, anchor_ref, limit_ref, hot_ref, acts_ref = refs
        hours = gap_ref.shape[0]
        unpack(hours, blocks, rows, packets_ref, anchor_ref, limit_ref, hot_ref, acts_ref)
        at = anchor_ref[...]
    elif kind == "middle":
        packets_ref, anchor_ref, limit_ref, hot_ref, acts_ref, before_ref, sums_ref, gap_ref, send_ref = refs
        at = moved(anchor_ref[...], before_ref[...], scale_of(sums_ref, entries))
    elif kind == "last":
        packets_ref, anchor_ref, limit_ref, hot_ref, acts_ref, lam_ref, before_ref, sums_ref, send_ref = refs
        at = moved(lam_ref[...], before_ref[...], scale_of(sums_ref, entries))
    else:
        packets_ref, anchor_ref, limit_ref, hot_ref, acts_ref = refs[:5]
        lam_ref, before_ref, sums_ref, gap_ref, send_ref, lam_out_ref = refs[5:]
        extra = moved(lam_ref[...], before_ref[...], scale_of(sums_ref, entries))
        weight = 1.0 / (kind + 2.0)
        at = weight * anchor_ref[...] + (1.0 - weight) * extra
        lam_out_ref[...] = at
    gap = usage_at(at, blocks, rows, packets_ref, hot_ref, acts_ref, *scratch) - limit_ref[...]
    line = jnp.sum(gap * gap, axis=0, keepdims=True)
    if kind != "last":
        gap_ref[...] = gap
        line = sum(line[:, n : n + TILE] for n in range(0, line.shape[1], TILE))
        send_ref[...] = jnp.broadcast_to(line[None], send_ref.shape)
        return
    hours, campaigns = gap.shape
    devices, span = send_ref.shape[:2]
    squares = jnp.broadcast_to(jnp.sum(line, axis=1, keepdims=True), (LINES, campaigns))
    results = [gap, lam_ref[...]]
    results.append(jnp.zeros((SUM_LANE - 2 * hours, campaigns), jnp.float32))
    results.append(squares)
    results.append(jnp.zeros((TILE - SUM_LANE - LINES, campaigns), jnp.float32))
    results = jnp.concatenate(results, axis=0).T
    for i in range(devices):
        send_ref[i] = results[i * span : (i + 1) * span]


def fold_kernel(last, parts_ref, out_ref):
    line = jnp.sum(parts_ref[:, 0, :], axis=0, keepdims=True)
    if last:
        lane = lax.broadcasted_iota(jnp.int32, line.shape, 1)
        line = jnp.where(lane == SUM_LANE, line, 0.0)
    out_ref[...] = jnp.broadcast_to(line[None], out_ref.shape)


def final_kernel(entries, step, anchor_ref, parts_ref, sums_ref, new_ref, dir_ref, rows):
    devices, span = parts_ref.shape[:2]
    hours, campaigns = anchor_ref.shape
    w = TILE // devices
    for m in range(devices):
        for j in range(span // w):
            rows[j * TILE + m * w : j * TILE + (m + 1) * w, :] = parts_ref[m, j * w : (j + 1) * w, :]
    results = rows[...].T
    gap, lam = results[:hours], results[hours : 2 * hours]
    scale = scale_of(sums_ref, entries)
    dir_ref[...] = gap * scale
    weight = 1.0 / (step + 2.0)
    new_ref[...] = weight * anchor_ref[...] + (1.0 - weight) * moved(lam, gap, scale)


def swapped(parts, axis):
    return lax.all_to_all(parts, axis, split_axis=0, concat_axis=0, tiled=True)


def kernel_call(body, name, out_shape, in_specs, out_specs, scratch_shapes=()):
    return pl.pallas_call(
        body,
        out_shape=out_shape,
        in_specs=in_specs,
        out_specs=out_specs,
        scratch_shapes=scratch_shapes,
        compiler_params=PARAMS,
        name=name,
    )


def on_device(scores, elig_ids, elig_counts, activity, prices, spend_limit):
    devices = lax.axis_size(USERS)
    groups = lax.axis_size("camps")
    entries = float(prices.size * devices * groups)
    hours, campaigns = prices.shape
    blocks, slots = scores.shape[0], scores.shape[2]
    w = TILE // devices
    span = campaigns // TILE * w
    rows = slots * w
    padded = pl.cdiv(blocks * rows, TILE) * TILE
    chunk = min(CHUNK, devices)
    bf16, f32, i32 = jnp.bfloat16, jnp.float32, jnp.int32
    shape = jax.ShapeDtypeStruct

    sources = (scores, elig_ids, elig_counts[:, 0], prices, spend_limit, activity)
    packets = kernel_call(
        cut_kernel,
        "cut",
        shape((devices, blocks * (rows + hours) + span, TILE), bf16),
        [HBM] * len(sources),
        VMEM,
        [
            pltpu.VMEM(scores.shape, bf16),
            pltpu.SMEM(elig_ids.shape, i32),
            pltpu.SMEM((blocks,), i32),
            pltpu.VMEM(prices.shape, f32),
            pltpu.VMEM(prices.shape, f32),
            pltpu.VMEM(activity.shape, bf16),
            pltpu.SemaphoreType.DMA((len(sources),)),
        ],
    )(*(pltpu.with_memory_space_constraint(source, pltpu.HBM) for source in sources))
    packets = swapped(packets, USERS)

    value = shape(prices.shape, f32)
    part = shape((devices, 1, TILE), f32)

    def total_of(parts, last=False):
        folded = kernel_call(
            functools.partial(fold_kernel, last), "fold", shape((groups, 1, TILE), f32), [VMEM], VMEM
        )(parts)
        return swapped(folded, "camps")

    def direction(kind, outs, *args):
        return kernel_call(
            functools.partial(direction_kernel, blocks, rows, entries, kind),
            "direction",
            outs,
            [VMEM] * len(args),
            [VMEM] * len(outs),
            [
                pltpu.VMEM((chunk, blocks * rows, blocks * ACT), bf16),
                pltpu.VMEM((chunk, TILE, padded), bf16),
                pltpu.VMEM((2 * ACT, chunk * padded), bf16),
            ],
        )(*args)

    kept_shapes = [
        value,
        value,
        shape((devices, padded, campaigns), bf16),
        shape((devices, blocks * ACT, TILE), bf16),
    ]
    gap, parts, *kept = direction("first", [value, part] + kept_shapes, packets)
    lam = kept[0]
    for step in range(STEPS - 1):
        sums = total_of(swapped(parts, USERS))
        gap, parts = direction("middle", [value, part], packets, *kept, gap, sums)
        sums = total_of(swapped(parts, USERS))
        gap, parts, lam = direction(step, [value, part, value], packets, *kept, lam, gap, sums)
    sums = total_of(swapped(parts, USERS))
    (parts,) = direction("last", [shape((devices, span, TILE), f32)], packets, *kept, lam, gap, sums)
    parts = swapped(parts, USERS)
    new, last = kernel_call(
        functools.partial(final_kernel, entries, STEPS - 1),
        "final",
        [value, value],
        [VMEM] * 3,
        [VMEM] * 2,
        [pltpu.VMEM((campaigns, TILE), f32)],
    )(prices, parts, total_of(parts, last=True))
    return (new, last)


def solution(mesh):
    torus = Mesh(
        mesh.devices.reshape(4, 4, 2, mesh.shape["camps"]),
        ("users_0", "users_1", "users_2", "camps"),
    )
    in_specs = (
        P(USERS, "camps", None, None, None),
        P(USERS, "camps", None),
        P(USERS, "camps"),
        P(None, USERS),
        P(None, USERS_CAMPS),
        P(None, USERS_CAMPS),
    )
    out_specs = (P(None, USERS_CAMPS), P(None, USERS_CAMPS))
    return jax.shard_map(
        on_device, mesh=torus, in_specs=in_specs, out_specs=out_specs, check_vma=False
    )
```

```python
import functools

import jax
import jax.numpy as jnp
from jax import lax
from jax.experimental import pallas as pl
from jax.experimental.pallas import tpu as pltpu
from jax.sharding import Mesh
from jax.sharding import PartitionSpec as P

STEPS = 2
USERS = ("users_0", "users_1", "users_2")
USERS_CAMPS = ("users_0", "users_1", "users_2", "camps")
TILE = 128
LINES = 8
TERMS = 5
ACT = 32
CHUNK = 32
UNROLL = 32
SUM_LANE = 64

VMEM = pl.BlockSpec(memory_space=pltpu.VMEM)
HBM = pl.BlockSpec(memory_space=pltpu.HBM)
PARAMS = pltpu.CompilerParams(vmem_limit_bytes=8 * 2**20)
TIGHT = pltpu.CompilerParams(vmem_limit_bytes=8 * 2**20)
NT = (((1,), (1,)), ((), ()))


def entry_place(hours, slots, block, slot):
    free = TILE - TERMS * hours
    return block * ((slots + free - 1) // free) + slot // free, TERMS * hours + slot % free


def rounded(value):
    return value.astype(jnp.bfloat16).astype(jnp.float32)


def cut_kernel(scores_hbm, ids_hbm, counts_hbm, prices_hbm, limit_hbm, act_hbm, out_ref, *scratch):
    scores, ids, counts, prices, limits, act, sems = scratch
    sources = (scores_hbm, ids_hbm, counts_hbm, prices_hbm, limit_hbm, act_hbm)
    loads = [pltpu.make_async_copy(sources[n], scratch[n], sems.at[n]) for n in range(len(sources))]
    for load in loads:
        load.start()
    devices = out_ref.shape[0]
    hours, campaigns = prices.shape
    blocks, slots = scores.shape[0], scores.shape[2]
    owned = campaigns // TILE
    w = TILE // devices
    span = owned * w
    acts = blocks * slots * w
    values = acts + blocks * hours
    row = lax.broadcasted_iota(jnp.int32, (campaigns, campaigns), 0)
    col = lax.broadcasted_iota(jnp.int32, (campaigns, campaigns), 1)
    source = lax.rem(row, span) // w * TILE + row // span * w + lax.rem(row, w)
    pick = jnp.where(col == source, 1.0, 0.0)
    pick_half = (pick * 0.5).astype(jnp.bfloat16)
    pick = pick.astype(jnp.bfloat16)

    loads[3].wait()
    loads[4].wait()
    price, limit = prices[...], limits[...]
    high = rounded(price)
    middle = rounded(price - high)
    limit_high = rounded(limit)
    terms = [high, middle, price - high - middle, limit_high, limit - limit_high]
    terms.append(jnp.zeros((TILE - len(terms) * hours, campaigns), jnp.float32))
    terms = jnp.concatenate(terms, axis=0).astype(jnp.bfloat16)
    terms = lax.dot_general(pick, terms, NT, preferred_element_type=jnp.float32)
    loads[1].wait()
    loads[2].wait()
    row = lax.broadcasted_iota(jnp.int32, (span, TILE), 0)
    lane = lax.broadcasted_iota(jnp.int32, (span, TILE), 1)
    entries = jnp.full((span, TILE), -TILE, jnp.int32)
    for b in range(blocks):
        for k in range(slots):
            at_row, at_lane = entry_place(hours, slots, b, k)
            here = jnp.logical_and(row == at_row, lane == at_lane)
            entries = jnp.where(here, jnp.where(k < counts[b], ids[b, 0, k] * w, -TILE), entries)
    entries = jnp.concatenate([entries.astype(jnp.float32)] * devices, axis=0)
    lane = lax.broadcasted_iota(jnp.int32, terms.shape, 1)
    terms = jnp.where(lane < TERMS * hours, terms, entries).astype(jnp.bfloat16)
    for m in range(devices):
        out_ref[m, values : values + span, :] = terms[m * span : (m + 1) * span]
    loads[5].wait()
    for b in range(blocks):
        own = act[:, b * TILE : (b + 1) * TILE]
        for m in range(devices):
            out_ref[m, acts + b * hours : acts + (b + 1) * hours, :] = own
    loads[0].wait()
    for b in range(blocks):
        for k in range(0, slots, owned):
            tiles = jnp.concatenate([scores[b, 0, k + j] for j in range(owned)], axis=1)
            cut = lax.dot_general(pick_half, tiles, NT, preferred_element_type=jnp.float32).astype(jnp.bfloat16)
            at = (b * slots + k) * w
            for m in range(devices):
                out_ref[m, at : at + span, :] = cut[m * span : (m + 1) * span]


def unpack(hours, blocks, rows, packets_ref, anchor_ref, limit_ref, hot_ref, acts_ref):
    devices = packets_ref.shape[0]
    campaigns = anchor_ref.shape[1]
    span = campaigns // devices
    w = TILE // devices
    act_row = blocks * rows
    values = act_row + blocks * hours
    slots = rows // w
    terms = packets_ref[:, values : values + span, :].reshape(campaigns, TILE).astype(jnp.float32).T
    terms = [terms[n * hours : (n + 1) * hours] for n in range(TERMS)]
    anchor_ref[...] = terms[0] + terms[1] + terms[2]
    limit_ref[...] = terms[3] + terms[4]
    hour = lax.broadcasted_iota(jnp.int32, (ACT - hours, TILE), 0)
    tail = jnp.where(hour == 0, 1.0, 0.0).astype(jnp.bfloat16)
    padded = hot_ref.shape[1]
    row = lax.broadcasted_iota(jnp.int32, (padded, TILE), 0)
    lane = lax.broadcasted_iota(jnp.int32, (padded, TILE), 1)
    at_row, at_lane = entry_place(hours, slots, row // rows, lax.rem(row, rows) // w)
    at_row = jnp.where(lane == at_lane, at_row, -1)
    lines = entry_place(hours, slots, blocks - 1, slots - 1)[0] + 1
    row = lax.broadcasted_iota(jnp.int32, (padded, campaigns), 0)
    wanted = lax.broadcasted_iota(jnp.int32, (padded, campaigns), 1) - lax.rem(row, w)
    wanted = jnp.where(row < blocks * rows, wanted, -2 * TILE).astype(jnp.float32)
    ones = jnp.ones((TILE, TILE), jnp.bfloat16)

    @pl.loop(0, devices // UNROLL)
    def _(step):
        for n in range(UNROLL):
            i = step * UNROLL + n
            ids = packets_ref[i, values : values + span, :].astype(jnp.float32)
            spread = jnp.zeros((padded, TILE), jnp.float32)
            for r in range(lines):
                spread = jnp.where(at_row == r, ids[r : r + 1, :], spread)
            for b in range(blocks):
                acts_ref[i, b * ACT : b * ACT + hours, :] = packets_ref[i, act_row + b * hours : act_row + (b + 1) * hours, :]
                acts_ref[i, b * ACT + hours : (b + 1) * ACT, :] = tail
            first = jnp.dot(spread.astype(jnp.bfloat16), ones, preferred_element_type=jnp.float32)
            first = jnp.concatenate([first] * (campaigns // TILE), axis=1)
            hot_ref[i] = jnp.where(first == wanted, 1.0, 0.0).astype(jnp.bfloat16)


def usage_at(lam, blocks, rows, packets_ref, hot_ref, acts_ref, named_ref, share_ref, used_ref):
    hours, campaigns = lam.shape
    devices, padded = hot_ref.shape[:2]
    chunk = share_ref.shape[0]
    listed = blocks * rows
    hour = lax.broadcasted_iota(jnp.int32, (ACT - hours, campaigns), 0)
    half = jnp.where(hour == 0, 0.5, 0.0)
    table = jnp.concatenate([rounded(lam) * -0.5, half] * blocks, axis=0).astype(jnp.bfloat16)
    row = lax.broadcasted_iota(jnp.int32, (listed, blocks * ACT), 0)
    own = row // rows == lax.broadcasted_iota(jnp.int32, (listed, blocks * ACT), 1) // ACT
    block = lax.broadcasted_iota(jnp.int32, (ACT, padded), 1) // rows
    if listed < padded:
        share_ref[:, :, listed:] = jnp.zeros((chunk, TILE, padded - listed), jnp.bfloat16)

    def senders(step, total):
        first = step * chunk
        hot = [hot_ref[first + n, :listed, :] for n in range(chunk)]
        for n in range(chunk):
            named = lax.dot_general(hot[n], table, NT, preferred_element_type=jnp.float32)
            named_ref[n] = jnp.where(own, named, 0.0).astype(jnp.bfloat16)
        for n in range(chunk):
            part = jnp.dot(named_ref[n], acts_ref[first + n], preferred_element_type=jnp.float32)
            score = packets_ref[first + n, :listed, :].astype(jnp.float32)
            share_ref[n, :, :listed] = jnp.clip(score + part, 0.0, 1.0).astype(jnp.bfloat16).T
        for n in range(chunk):
            each = jnp.dot(acts_ref[first + n], share_ref[n], preferred_element_type=jnp.float32)
            used = each[:ACT]
            for b in range(1, blocks):
                used = jnp.where(block == b, each[b * ACT : (b + 1) * ACT], used)
            high = rounded(used)
            both = jnp.concatenate([high, used - high], axis=0).astype(jnp.bfloat16)
            used_ref[:, n * padded : (n + 1) * padded] = both
        hot = hot_ref[pl.ds(first, chunk)].reshape(chunk * padded, campaigns)
        return total + jnp.dot(used_ref[...], hot, preferred_element_type=jnp.float32)

    total = jnp.zeros((2 * ACT, campaigns), jnp.float32)
    total = lax.fori_loop(0, devices // chunk, senders, total)
    return total[:hours] + total[ACT : ACT + hours]


def scale_of(parts_ref, entries):
    squares = jnp.sum(jnp.sum(parts_ref[:, 0, :], axis=0, keepdims=True), axis=1, keepdims=True)
    return lax.rsqrt(squares / entries + 1e-06)


def moved(lam, gap, scale):
    return jnp.maximum(lam + 0.3 * (gap * scale), 0.0)


def direction_kernel(blocks, rows, entries, kind, *refs):
    refs, scratch = refs[:-3], refs[-3:]
    if kind == "first":
        packets_ref, gap_ref, send_ref, anchor_ref, limit_ref, hot_ref, acts_ref = refs
        hours = gap_ref.shape[0]
        unpack(hours, blocks, rows, packets_ref, anchor_ref, limit_ref, hot_ref, acts_ref)
        at = anchor_ref[...]
    elif kind == "middle":
        packets_ref, anchor_ref, limit_ref, hot_ref, acts_ref, before_ref, sums_ref, gap_ref, send_ref = refs
        at = moved(anchor_ref[...], before_ref[...], scale_of(sums_ref, entries))
    elif kind == "last":
        packets_ref, anchor_ref, limit_ref, hot_ref, acts_ref, lam_ref, before_ref, sums_ref, send_ref = refs
        at = moved(lam_ref[...], before_ref[...], scale_of(sums_ref, entries))
    else:
        packets_ref, anchor_ref, limit_ref, hot_ref, acts_ref = refs[:5]
        lam_ref, before_ref, sums_ref, gap_ref, send_ref, lam_out_ref = refs[5:]
        extra = moved(lam_ref[...], before_ref[...], scale_of(sums_ref, entries))
        weight = 1.0 / (kind + 2.0)
        at = weight * anchor_ref[...] + (1.0 - weight) * extra
        lam_out_ref[...] = at
    gap = usage_at(at, blocks, rows, packets_ref, hot_ref, acts_ref, *scratch) - limit_ref[...]
    line = jnp.sum(gap * gap, axis=0, keepdims=True)
    if kind != "last":
        gap_ref[...] = gap
        line = sum(line[:, n : n + TILE] for n in range(0, line.shape[1], TILE))
        send_ref[...] = jnp.broadcast_to(line[None], send_ref.shape)
        return
    hours, campaigns = gap.shape
    devices, span = send_ref.shape[:2]
    squares = jnp.broadcast_to(jnp.sum(line, axis=1, keepdims=True), (LINES, campaigns))
    results = [gap, lam_ref[...]]
    results.append(jnp.zeros((SUM_LANE - 2 * hours, campaigns), jnp.float32))
    results.append(squares)
    results.append(jnp.zeros((TILE - SUM_LANE - LINES, campaigns), jnp.float32))
    results = jnp.concatenate(results, axis=0).T
    for i in range(devices):
        send_ref[i] = results[i * span : (i + 1) * span]


def fold_kernel(last, parts_ref, out_ref):
    line = jnp.sum(parts_ref[:, 0, :], axis=0, keepdims=True)
    if last:
        lane = lax.broadcasted_iota(jnp.int32, line.shape, 1)
        line = jnp.where(lane == SUM_LANE, line, 0.0)
    out_ref[...] = jnp.broadcast_to(line[None], out_ref.shape)


def final_kernel(entries, step, anchor_ref, parts_ref, sums_ref, new_ref, dir_ref, rows):
    devices, span = parts_ref.shape[:2]
    hours, campaigns = anchor_ref.shape
    w = TILE // devices
    for m in range(devices):
        for j in range(span // w):
            rows[j * TILE + m * w : j * TILE + (m + 1) * w, :] = parts_ref[m, j * w : (j + 1) * w, :]
    results = rows[...].T
    gap, lam = results[:hours], results[hours : 2 * hours]
    scale = scale_of(sums_ref, entries)
    dir_ref[...] = gap * scale
    weight = 1.0 / (step + 2.0)
    new_ref[...] = weight * anchor_ref[...] + (1.0 - weight) * moved(lam, gap, scale)


def swapped(parts, axis):
    return lax.all_to_all(parts, axis, split_axis=0, concat_axis=0, tiled=True)


def kernel_call(body, name, out_shape, in_specs, out_specs, scratch_shapes=(), params=PARAMS):
    return pl.pallas_call(
        body,
        out_shape=out_shape,
        in_specs=in_specs,
        out_specs=out_specs,
        scratch_shapes=scratch_shapes,
        compiler_params=params,
        name=name,
    )


def on_device(scores, elig_ids, elig_counts, activity, prices, spend_limit):
    devices = lax.axis_size(USERS)
    groups = lax.axis_size("camps")
    entries = float(prices.size * devices * groups)
    hours, campaigns = prices.shape
    blocks, slots = scores.shape[0], scores.shape[2]
    w = TILE // devices
    span = campaigns // TILE * w
    rows = slots * w
    padded = pl.cdiv(blocks * rows, TILE) * TILE
    chunk = min(CHUNK, devices)
    bf16, f32, i32 = jnp.bfloat16, jnp.float32, jnp.int32
    shape = jax.ShapeDtypeStruct

    sources = (scores, elig_ids, elig_counts[:, 0], prices, spend_limit, activity)
    packets = kernel_call(
        cut_kernel,
        "cut",
        shape((devices, blocks * (rows + hours) + span, TILE), bf16),
        [HBM] * len(sources),
        VMEM,
        [
            pltpu.VMEM(scores.shape, bf16),
            pltpu.SMEM(elig_ids.shape, i32),
            pltpu.SMEM((blocks,), i32),
            pltpu.VMEM(prices.shape, f32),
            pltpu.VMEM(prices.shape, f32),
            pltpu.VMEM(activity.shape, bf16),
            pltpu.SemaphoreType.DMA((len(sources),)),
        ],
    )(*(pltpu.with_memory_space_constraint(source, pltpu.HBM) for source in sources))
    packets = swapped(packets, USERS)

    value = shape(prices.shape, f32)
    part = shape((devices, 1, TILE), f32)

    def total_of(parts, last=False):
        folded = kernel_call(
            functools.partial(fold_kernel, last), "fold", shape((groups, 1, TILE), f32), [VMEM], VMEM
        )(parts)
        return swapped(folded, "camps")

    def direction(kind, outs, *args):
        return kernel_call(
            functools.partial(direction_kernel, blocks, rows, entries, kind),
            "direction",
            outs,
            [VMEM] * len(args),
            [VMEM] * len(outs),
            [
                pltpu.VMEM((chunk, blocks * rows, blocks * ACT), bf16),
                pltpu.VMEM((chunk, TILE, padded), bf16),
                pltpu.VMEM((2 * ACT, chunk * padded), bf16),
            ],
            PARAMS if kind == "first" else TIGHT,
        )(*args)

    kept_shapes = [
        value,
        value,
        shape((devices, padded, campaigns), bf16),
        shape((devices, blocks * ACT, TILE), bf16),
    ]
    gap, parts, *kept = direction("first", [value, part] + kept_shapes, packets)
    lam = kept[0]
    for step in range(STEPS - 1):
        sums = total_of(swapped(parts, USERS))
        gap, parts = direction("middle", [value, part], packets, *kept, gap, sums)
        sums = total_of(swapped(parts, USERS))
        gap, parts, lam = direction(step, [value, part, value], packets, *kept, lam, gap, sums)
    sums = total_of(swapped(parts, USERS))
    (parts,) = direction("last", [shape((devices, span, TILE), f32)], packets, *kept, lam, gap, sums)
    parts = swapped(parts, USERS)
    new, last = kernel_call(
        functools.partial(final_kernel, entries, STEPS - 1),
        "final",
        [value, value],
        [VMEM] * 3,
        [VMEM] * 2,
        [pltpu.VMEM((campaigns, TILE), f32)],
    )(prices, parts, total_of(parts, last=True))
    return (new, last)


def solution(mesh):
    torus = Mesh(
        mesh.devices.reshape(4, 4, 2, mesh.shape["camps"]),
        ("users_0", "users_1", "users_2", "camps"),
    )
    in_specs = (
        P(USERS, "camps", None, None, None),
        P(USERS, "camps", None),
        P(USERS, "camps"),
        P(None, USERS),
        P(None, USERS_CAMPS),
        P(None, USERS_CAMPS),
    )
    out_specs = (P(None, USERS_CAMPS), P(None, USERS_CAMPS))
    return jax.shard_map(
        on_device, mesh=torus, in_specs=in_specs, out_specs=out_specs, check_vma=False
    )
```

```python
import functools

import jax
import jax.numpy as jnp
from jax import lax
from jax.experimental import pallas as pl
from jax.experimental.pallas import tpu as pltpu
from jax.sharding import Mesh
from jax.sharding import PartitionSpec as P

STEPS = 2
USERS = ("users_0", "users_1", "users_2")
USERS_CAMPS = ("users_0", "users_1", "users_2", "camps")
TILE = 128
LINES = 8
TERMS = 5
ACT = 32
CHUNK = 32
UNROLL = 32
SUM_LANE = 64

VMEM = pl.BlockSpec(memory_space=pltpu.VMEM)
HBM = pl.BlockSpec(memory_space=pltpu.HBM)
PARAMS = pltpu.CompilerParams(vmem_limit_bytes=8 * 2**20)
TIGHT = pltpu.CompilerParams(vmem_limit_bytes=8 * 2**20)
NT = (((1,), (1,)), ((), ()))


def entry_place(hours, slots, block, slot):
    free = TILE - TERMS * hours
    return block * ((slots + free - 1) // free) + slot // free, TERMS * hours + slot % free


def rounded(value):
    return value.astype(jnp.bfloat16).astype(jnp.float32)


def cut_kernel(scores_hbm, ids_hbm, counts_hbm, prices_hbm, limit_hbm, act_hbm, out_ref, *scratch):
    scores, ids, counts, prices, limits, act, sems = scratch
    sources = (scores_hbm, ids_hbm, counts_hbm, prices_hbm, limit_hbm, act_hbm)
    loads = [pltpu.make_async_copy(sources[n], scratch[n], sems.at[n]) for n in range(1, len(sources))]
    for b in range(scores.shape[0]):
        loads.append(pltpu.make_async_copy(scores_hbm.at[b], scores.at[b], sems.at[len(loads) + 1]))
    for load in loads:
        load.start()
    devices = out_ref.shape[0]
    hours, campaigns = prices.shape
    blocks, slots = scores.shape[0], scores.shape[2]
    owned = campaigns // TILE
    w = TILE // devices
    span = owned * w
    acts = blocks * slots * w
    values = acts + blocks * hours
    row = lax.broadcasted_iota(jnp.int32, (campaigns, campaigns), 0)
    col = lax.broadcasted_iota(jnp.int32, (campaigns, campaigns), 1)
    source = lax.rem(row, span) // w * TILE + row // span * w + lax.rem(row, w)
    pick = jnp.where(col == source, 1.0, 0.0)
    pick_half = (pick * 0.5).astype(jnp.bfloat16)
    pick = pick.astype(jnp.bfloat16)

    loads[2].wait()
    loads[3].wait()
    price, limit = prices[...], limits[...]
    high = rounded(price)
    middle = rounded(price - high)
    limit_high = rounded(limit)
    terms = [high, middle, price - high - middle, limit_high, limit - limit_high]
    terms.append(jnp.zeros((TILE - len(terms) * hours, campaigns), jnp.float32))
    terms = jnp.concatenate(terms, axis=0).astype(jnp.bfloat16)
    terms = lax.dot_general(pick, terms, NT, preferred_element_type=jnp.float32)
    loads[0].wait()
    loads[1].wait()
    row = lax.broadcasted_iota(jnp.int32, (span, TILE), 0)
    lane = lax.broadcasted_iota(jnp.int32, (span, TILE), 1)
    entries = jnp.full((span, TILE), -TILE, jnp.int32)
    for b in range(blocks):
        for k in range(slots):
            at_row, at_lane = entry_place(hours, slots, b, k)
            here = jnp.logical_and(row == at_row, lane == at_lane)
            entries = jnp.where(here, jnp.where(k < counts[b], ids[b, 0, k] * w, -TILE), entries)
    entries = jnp.concatenate([entries.astype(jnp.float32)] * devices, axis=0)
    lane = lax.broadcasted_iota(jnp.int32, terms.shape, 1)
    terms = jnp.where(lane < TERMS * hours, terms, entries).astype(jnp.bfloat16)
    for m in range(devices):
        out_ref[m, values : values + span, :] = terms[m * span : (m + 1) * span]
    loads[4].wait()
    for b in range(blocks):
        own = act[:, b * TILE : (b + 1) * TILE]
        for m in range(devices):
            out_ref[m, acts + b * hours : acts + (b + 1) * hours, :] = own
    for b in range(blocks):
        loads[len(sources) - 1 + b].wait()
        for k in range(0, slots, owned):
            tiles = jnp.concatenate([scores[b, 0, k + j] for j in range(owned)], axis=1)
            cut = lax.dot_general(pick_half, tiles, NT, preferred_element_type=jnp.float32).astype(jnp.bfloat16)
            at = (b * slots + k) * w
            for m in range(devices):
                out_ref[m, at : at + span, :] = cut[m * span : (m + 1) * span]


def unpack(hours, blocks, rows, packets_ref, anchor_ref, limit_ref, hot_ref, acts_ref):
    devices = packets_ref.shape[0]
    campaigns = anchor_ref.shape[1]
    span = campaigns // devices
    w = TILE // devices
    act_row = blocks * rows
    values = act_row + blocks * hours
    slots = rows // w
    terms = packets_ref[:, values : values + span, :].reshape(campaigns, TILE).astype(jnp.float32).T
    terms = [terms[n * hours : (n + 1) * hours] for n in range(TERMS)]
    anchor_ref[...] = terms[0] + terms[1] + terms[2]
    limit_ref[...] = terms[3] + terms[4]
    hour = lax.broadcasted_iota(jnp.int32, (ACT - hours, TILE), 0)
    tail = jnp.where(hour == 0, 1.0, 0.0).astype(jnp.bfloat16)
    padded = hot_ref.shape[1]
    row = lax.broadcasted_iota(jnp.int32, (padded, TILE), 0)
    lane = lax.broadcasted_iota(jnp.int32, (padded, TILE), 1)
    at_row, at_lane = entry_place(hours, slots, row // rows, lax.rem(row, rows) // w)
    at_row = jnp.where(lane == at_lane, at_row, -1)
    lines = entry_place(hours, slots, blocks - 1, slots - 1)[0] + 1
    row = lax.broadcasted_iota(jnp.int32, (padded, campaigns), 0)
    wanted = lax.broadcasted_iota(jnp.int32, (padded, campaigns), 1) - lax.rem(row, w)
    wanted = jnp.where(row < blocks * rows, wanted, -2 * TILE).astype(jnp.float32)
    ones = jnp.ones((TILE, TILE), jnp.bfloat16)

    @pl.loop(0, devices // UNROLL)
    def _(step):
        for n in range(UNROLL):
            i = step * UNROLL + n
            ids = packets_ref[i, values : values + span, :].astype(jnp.float32)
            spread = jnp.zeros((padded, TILE), jnp.float32)
            for r in range(lines):
                spread = jnp.where(at_row == r, ids[r : r + 1, :], spread)
            for b in range(blocks):
                acts_ref[i, b * ACT : b * ACT + hours, :] = packets_ref[i, act_row + b * hours : act_row + (b + 1) * hours, :]
                acts_ref[i, b * ACT + hours : (b + 1) * ACT, :] = tail
            first = jnp.dot(spread.astype(jnp.bfloat16), ones, preferred_element_type=jnp.float32)
            first = jnp.concatenate([first] * (campaigns // TILE), axis=1)
            hot_ref[i] = jnp.where(first == wanted, 1.0, 0.0).astype(jnp.bfloat16)


def usage_at(lam, blocks, rows, packets_ref, hot_ref, acts_ref, named_ref, share_ref, used_ref):
    hours, campaigns = lam.shape
    devices, padded = hot_ref.shape[:2]
    chunk = share_ref.shape[0]
    listed = blocks * rows
    hour = lax.broadcasted_iota(jnp.int32, (ACT - hours, campaigns), 0)
    half = jnp.where(hour == 0, 0.5, 0.0)
    table = jnp.concatenate([rounded(lam) * -0.5, half] * blocks, axis=0).astype(jnp.bfloat16)
    row = lax.broadcasted_iota(jnp.int32, (listed, blocks * ACT), 0)
    own = row // rows == lax.broadcasted_iota(jnp.int32, (listed, blocks * ACT), 1) // ACT
    block = lax.broadcasted_iota(jnp.int32, (ACT, padded), 1) // rows
    if listed < padded:
        share_ref[:, :, listed:] = jnp.zeros((chunk, TILE, padded - listed), jnp.bfloat16)

    def senders(step, total):
        first = step * chunk
        hot = [hot_ref[first + n, :listed, :] for n in range(chunk)]
        for n in range(chunk):
            named = lax.dot_general(hot[n], table, NT, preferred_element_type=jnp.float32)
            named_ref[n] = jnp.where(own, named, 0.0).astype(jnp.bfloat16)
        for n in range(chunk):
            part = jnp.dot(named_ref[n], acts_ref[first + n], preferred_element_type=jnp.float32)
            score = packets_ref[first + n, :listed, :].astype(jnp.float32)
            share_ref[n, :, :listed] = jnp.clip(score + part, 0.0, 1.0).astype(jnp.bfloat16).T
        for n in range(chunk):
            each = jnp.dot(acts_ref[first + n], share_ref[n], preferred_element_type=jnp.float32)
            used = each[:ACT]
            for b in range(1, blocks):
                used = jnp.where(block == b, each[b * ACT : (b + 1) * ACT], used)
            high = rounded(used)
            both = jnp.concatenate([high, used - high], axis=0).astype(jnp.bfloat16)
            used_ref[:, n * padded : (n + 1) * padded] = both
        hot = hot_ref[pl.ds(first, chunk)].reshape(chunk * padded, campaigns)
        return total + jnp.dot(used_ref[...], hot, preferred_element_type=jnp.float32)

    total = jnp.zeros((2 * ACT, campaigns), jnp.float32)
    total = lax.fori_loop(0, devices // chunk, senders, total)
    return total[:hours] + total[ACT : ACT + hours]


def scale_of(parts_ref, entries):
    squares = jnp.sum(jnp.sum(parts_ref[:, 0, :], axis=0, keepdims=True), axis=1, keepdims=True)
    return lax.rsqrt(squares / entries + 1e-06)


def moved(lam, gap, scale):
    return jnp.maximum(lam + 0.3 * (gap * scale), 0.0)


def direction_kernel(blocks, rows, entries, kind, *refs):
    refs, scratch = refs[:-3], refs[-3:]
    if kind == "first":
        packets_ref, gap_ref, send_ref, anchor_ref, limit_ref, hot_ref, acts_ref = refs
        hours = gap_ref.shape[0]
        unpack(hours, blocks, rows, packets_ref, anchor_ref, limit_ref, hot_ref, acts_ref)
        at = anchor_ref[...]
    elif kind == "middle":
        packets_ref, anchor_ref, limit_ref, hot_ref, acts_ref, before_ref, sums_ref, gap_ref, send_ref = refs
        at = moved(anchor_ref[...], before_ref[...], scale_of(sums_ref, entries))
    elif kind == "last":
        packets_ref, anchor_ref, limit_ref, hot_ref, acts_ref, lam_ref, before_ref, sums_ref, send_ref = refs
        at = moved(lam_ref[...], before_ref[...], scale_of(sums_ref, entries))
    else:
        packets_ref, anchor_ref, limit_ref, hot_ref, acts_ref = refs[:5]
        lam_ref, before_ref, sums_ref, gap_ref, send_ref, lam_out_ref = refs[5:]
        extra = moved(lam_ref[...], before_ref[...], scale_of(sums_ref, entries))
        weight = 1.0 / (kind + 2.0)
        at = weight * anchor_ref[...] + (1.0 - weight) * extra
        lam_out_ref[...] = at
    gap = usage_at(at, blocks, rows, packets_ref, hot_ref, acts_ref, *scratch) - limit_ref[...]
    line = jnp.sum(gap * gap, axis=0, keepdims=True)
    if kind != "last":
        gap_ref[...] = gap
        line = sum(line[:, n : n + TILE] for n in range(0, line.shape[1], TILE))
        send_ref[...] = jnp.broadcast_to(line[None], send_ref.shape)
        return
    hours, campaigns = gap.shape
    devices, span = send_ref.shape[:2]
    squares = jnp.broadcast_to(jnp.sum(line, axis=1, keepdims=True), (LINES, campaigns))
    results = [gap, lam_ref[...]]
    results.append(jnp.zeros((SUM_LANE - 2 * hours, campaigns), jnp.float32))
    results.append(squares)
    results.append(jnp.zeros((TILE - SUM_LANE - LINES, campaigns), jnp.float32))
    results = jnp.concatenate(results, axis=0).T
    for i in range(devices):
        send_ref[i] = results[i * span : (i + 1) * span]


def fold_kernel(last, parts_ref, out_ref):
    line = jnp.sum(parts_ref[:, 0, :], axis=0, keepdims=True)
    if last:
        lane = lax.broadcasted_iota(jnp.int32, line.shape, 1)
        line = jnp.where(lane == SUM_LANE, line, 0.0)
    out_ref[...] = jnp.broadcast_to(line[None], out_ref.shape)


def final_kernel(entries, step, anchor_ref, parts_ref, sums_ref, new_ref, dir_ref, rows):
    devices, span = parts_ref.shape[:2]
    hours, campaigns = anchor_ref.shape
    w = TILE // devices
    for m in range(devices):
        for j in range(span // w):
            rows[j * TILE + m * w : j * TILE + (m + 1) * w, :] = parts_ref[m, j * w : (j + 1) * w, :]
    results = rows[...].T
    gap, lam = results[:hours], results[hours : 2 * hours]
    scale = scale_of(sums_ref, entries)
    dir_ref[...] = gap * scale
    weight = 1.0 / (step + 2.0)
    new_ref[...] = weight * anchor_ref[...] + (1.0 - weight) * moved(lam, gap, scale)


def swapped(parts, axis):
    return lax.all_to_all(parts, axis, split_axis=0, concat_axis=0, tiled=True)


def kernel_call(body, name, out_shape, in_specs, out_specs, scratch_shapes=(), params=PARAMS):
    return pl.pallas_call(
        body,
        out_shape=out_shape,
        in_specs=in_specs,
        out_specs=out_specs,
        scratch_shapes=scratch_shapes,
        compiler_params=params,
        name=name,
    )


def on_device(scores, elig_ids, elig_counts, activity, prices, spend_limit):
    devices = lax.axis_size(USERS)
    groups = lax.axis_size("camps")
    entries = float(prices.size * devices * groups)
    hours, campaigns = prices.shape
    blocks, slots = scores.shape[0], scores.shape[2]
    w = TILE // devices
    span = campaigns // TILE * w
    rows = slots * w
    padded = pl.cdiv(blocks * rows, TILE) * TILE
    chunk = min(CHUNK, devices)
    bf16, f32, i32 = jnp.bfloat16, jnp.float32, jnp.int32
    shape = jax.ShapeDtypeStruct

    sources = (scores, elig_ids, elig_counts[:, 0], prices, spend_limit, activity)
    packets = kernel_call(
        cut_kernel,
        "cut",
        shape((devices, blocks * (rows + hours) + span, TILE), bf16),
        [HBM] * len(sources),
        VMEM,
        [
            pltpu.VMEM(scores.shape, bf16),
            pltpu.SMEM(elig_ids.shape, i32),
            pltpu.SMEM((blocks,), i32),
            pltpu.VMEM(prices.shape, f32),
            pltpu.VMEM(prices.shape, f32),
            pltpu.VMEM(activity.shape, bf16),
            pltpu.SemaphoreType.DMA((len(sources) + blocks,)),
        ],
    )(*(pltpu.with_memory_space_constraint(source, pltpu.HBM) for source in sources))
    packets = swapped(packets, USERS)

    value = shape(prices.shape, f32)
    part = shape((devices, 1, TILE), f32)

    def total_of(parts, last=False):
        folded = kernel_call(
            functools.partial(fold_kernel, last), "fold", shape((groups, 1, TILE), f32), [VMEM], VMEM
        )(parts)
        return swapped(folded, "camps")

    def direction(kind, outs, *args):
        return kernel_call(
            functools.partial(direction_kernel, blocks, rows, entries, kind),
            "direction",
            outs,
            [VMEM] * len(args),
            [VMEM] * len(outs),
            [
                pltpu.VMEM((chunk, blocks * rows, blocks * ACT), bf16),
                pltpu.VMEM((chunk, TILE, padded), bf16),
                pltpu.VMEM((2 * ACT, chunk * padded), bf16),
            ],
            PARAMS if kind == "first" else TIGHT,
        )(*args)

    kept_shapes = [
        value,
        value,
        shape((devices, padded, campaigns), bf16),
        shape((devices, blocks * ACT, TILE), bf16),
    ]
    gap, parts, *kept = direction("first", [value, part] + kept_shapes, packets)
    lam = kept[0]
    for step in range(STEPS - 1):
        sums = total_of(swapped(parts, USERS))
        gap, parts = direction("middle", [value, part], packets, *kept, gap, sums)
        sums = total_of(swapped(parts, USERS))
        gap, parts, lam = direction(step, [value, part, value], packets, *kept, lam, gap, sums)
    sums = total_of(swapped(parts, USERS))
    (parts,) = direction("last", [shape((devices, span, TILE), f32)], packets, *kept, lam, gap, sums)
    parts = swapped(parts, USERS)
    new, last = kernel_call(
        functools.partial(final_kernel, entries, STEPS - 1),
        "final",
        [value, value],
        [VMEM] * 3,
        [VMEM] * 2,
        [pltpu.VMEM((campaigns, TILE), f32)],
    )(prices, parts, total_of(parts, last=True))
    return (new, last)


def solution(mesh):
    torus = Mesh(
        mesh.devices.reshape(4, 4, 2, mesh.shape["camps"]),
        ("users_0", "users_1", "users_2", "camps"),
    )
    in_specs = (
        P(USERS, "camps", None, None, None),
        P(USERS, "camps", None),
        P(USERS, "camps"),
        P(None, USERS),
        P(None, USERS_CAMPS),
        P(None, USERS_CAMPS),
    )
    out_specs = (P(None, USERS_CAMPS), P(None, USERS_CAMPS))
    return jax.shard_map(
        on_device, mesh=torus, in_specs=in_specs, out_specs=out_specs, check_vma=False
    )
```
